256 devices in a mesh: shot: 8 (over y, z_lo), space: 32 (over x, z_hi, core).
Axes of the slice: x: 4, y: 4, z: 8 (z_hi: 4, z_lo: 2; z = z_hi * 2 + z_lo), core: 2. Of those that a mesh axis runs over, the one named last changes fastest.
Arguments:
- wave_prev: float32 [8, 512, 128, 128], P('shot', 'space'), may hold values from -6 to 6
- wave_now: float32 [8, 512, 128, 128], P('shot', 'space'), may hold values from -6 to 6
- velocity: float32 [512, 128, 128], P('space'), may hold values from 0.05 to 0.2
- probe_panel: float32 [4, 512, 128, 128], P(None, 'space', 'shot'), may hold values from -6 to 6
- source_depth: int32 [8], P('shot'), may hold values from 0 to 511
- source_column: int32 [8], P('shot'), may hold values from 0 to 16383
- source_strength: float32 [8], P('shot'), may hold values from 2 to 6
- receiver_wells: int32 [8, 512], P('shot'), may hold values from 0 to 16383
Outputs:
- hessian_action: float32 [4, 512, 128, 128], P(None, 'space', 'shot')
The draws below stay inside these ranges and needn't reach their ends.
All inputs are finite; a program needn't handle non-finite values.
Results may differ from the reference program's by a relative error of at most 0.0003.
Values sent between devices are 32-bit elements; how exact they have to be, the bound alone decides.
No kernel may reach another device: no remote copies, remote signals or barrier semaphores. Data moves between devices by JAX's collectives and lax.ppermute only.
A program may use at most 128 MiB of HBM per device.

```python
import jax
import jax.numpy as jnp
from jax import lax

NPROBE = 4
NX = 128
NY = 128
REC = 512
NZ = 512
SHOTS = 8


def touch_ends(array, own_key, least, largest):
    shape = array.shape
    place = [jax.random.randint(jax.random.fold_in(own_key, axis), (), 0, shape[axis]) for axis in range(len(shape))]
    array = array.at[tuple(place)].set(least)
    longest = shape.index(max(shape))
    place[longest] = (place[longest] + 1) % shape[longest]
    return array.at[tuple(place)].set(largest)


def levels(key, dims, cuts, least, top_value):
    loudness = 1.0
    for dim, blocks in cuts:
        heights = jax.random.uniform(jax.random.fold_in(jax.random.fold_in(key, 6), dim), (blocks,), jnp.float32, least / len(cuts), top_value / len(cuts))
        loudness = loudness * jnp.repeat(jnp.exp(heights), dims[dim] // blocks).reshape((-1,) + (1,) * (len(dims) - 1 - dim))
    return loudness


def gaussian(stream_key, shape, spread, limit, pieces=(), kind=jnp.bfloat16):
    array = jax.random.normal(stream_key, shape, jnp.float32) * spread
    if len(pieces) > 0:
        array = levels(stream_key, shape, pieces, -0.22, 0.18) * array
    return jnp.clip(array, min=-limit, max=limit).astype(kind)


def setup_inputs(seed: int = 0) -> dict:
    seeds = jax.random.split(jax.random.key(seed), 9)
    return {
        "wave_prev": gaussian(seeds[0], (SHOTS, NZ, NX, NY), 1.0, 6.0, ((0, 8), (1, 32)), jnp.float32),
        "wave_now": gaussian(seeds[1], (SHOTS, NZ, NX, NY), 1.0, 6.0, ((0, 8), (1, 32)), jnp.float32),
        "velocity": jnp.clip(0.05 + 0.15 * jax.random.uniform(seeds[2], (NZ, NX, NY), jnp.float32) ** levels(seeds[2], (NZ, NX, NY), ((0, 32),), -0.2, 0.2), 0.05, 0.2),
        "probe_panel": gaussian(seeds[3], (NPROBE, NZ, NX, NY), 1.0, 6.0, ((1, 32), (2, 8)), jnp.float32),
        "source_depth": touch_ends(jax.random.randint(seeds[4], (SHOTS,), 0, NZ), jax.random.fold_in(seeds[4], 1), 0, NZ - 1).astype(jnp.int32),
        "source_column": touch_ends(jax.random.randint(seeds[5], (SHOTS,), 0, NX * NY), jax.random.fold_in(seeds[5], 1), 0, (NX * NY) - 1).astype(jnp.int32),
        "source_strength": jnp.clip(2.0 + 4.0 * jax.random.uniform(seeds[6], (SHOTS,), jnp.float32) ** levels(seeds[6], (SHOTS,), ((0, 8),), -0.2, 0.2), 2.0, 6.0),
        "receiver_wells": touch_ends(jax.random.randint(seeds[7], (SHOTS, REC), 0, NX * NY), jax.random.fold_in(seeds[7], 1), 0, (NX * NY) - 1).astype(jnp.int32),
    }


CENTER = -205.0 / 72.0
WEIGHTS = (8.0 / 5.0, -1.0 / 5.0, 8.0 / 315.0, -1.0 / 560.0)


def laplace(padded):
    count_rows = padded.shape[-3] - 8
    middle = padded[..., 4:4 + count_rows, :, :]
    count_x = middle.shape[-2]
    count_y = middle.shape[-1]
    lead_pads = [(0, 0)] * (middle.ndim - 2)
    wide_x = jnp.pad(middle, lead_pads + [(4, 4), (0, 0)])
    wide_y = jnp.pad(middle, lead_pads + [(0, 0), (4, 4)])
    stencil = (3.0 * CENTER) * middle
    for offset in range(1, 5):
        weight = WEIGHTS[offset - 1]
        stencil = stencil + weight * (padded[..., 4 + offset:4 + offset + count_rows, :, :] + padded[..., 4 - offset:4 - offset + count_rows, :, :])
        stencil = stencil + weight * (wide_x[..., 4 + offset:4 + offset + count_x, :] + wide_x[..., 4 - offset:4 - offset + count_x, :])
        stencil = stencil + weight * (wide_y[..., 4 + offset:4 + offset + count_y] + wide_y[..., 4 - offset:4 - offset + count_y])
    return stencil


def zero_rim(field):
    return jnp.pad(field, [(0, 0)] * (field.ndim - 3) + [(4, 4), (0, 0), (0, 0)])


def reference(wave_prev, wave_now, velocity, probe_panel, source_depth, source_column, source_strength, receiver_wells):
    depth_ids = jnp.arange(NZ, dtype=jnp.int32)
    column_ids = jnp.arange(NX * NY, dtype=jnp.int32).reshape(NX, NY)

    def one_shot(carry, items):
        prev_field, now_field, depth, column, strength, wells = items
        born_zero = velocity * laplace(zero_rim(now_field))
        source_mark = ((depth_ids == depth)[:, None, None] & (column_ids == column)[None, :, :]).astype(jnp.float32)
        upcoming = 2.0 * now_field - prev_field + born_zero + source_mark * strength
        born_one = velocity * laplace(zero_rim(upcoming))
        first_field = probe_panel * born_zero
        second_field = 2.0 * first_field + velocity * laplace(zero_rim(first_field)) + probe_panel * born_one
        counts = jnp.zeros((NX * NY,), jnp.float32).at[wells].add(1.0).reshape(NX, NY)
        late_field = counts * second_field
        early_field = counts * first_field + 2.0 * late_field + laplace(zero_rim(velocity * late_field))
        return carry + (born_zero * early_field + born_one * late_field), None

    start = jnp.zeros((NPROBE, NZ, NX, NY), jnp.float32)
    summed, unused = lax.scan(one_shot, start, (wave_prev, wave_now, source_depth, source_column, source_strength, receiver_wells))
    return summed / SHOTS
```

```python
import functools

import jax
import jax.numpy as jnp
from jax import lax
from jax.experimental import pallas as pl
from jax.experimental.pallas import tpu as pltpu
from jax.sharding import PartitionSpec as P


CENTER = 3.0 * (-205.0 / 72.0)
WEIGHTS = (8.0 / 5.0, -1.0 / 5.0, 8.0 / 315.0, -1.0 / 560.0)
SCALE = WEIGHTS[0]
RATIOS = tuple(w / SCALE for w in WEIGHTS)
F32 = jnp.float32
BF16 = jnp.bfloat16


def halves(value):
    high = value.astype(BF16)
    low = (value - high.astype(F32)).astype(BF16)
    return high, low


def band(distance):
    out = jnp.zeros(distance.shape, F32)
    for k in range(1, 5):
        out = jnp.where(distance == k, RATIOS[k - 1], out)
    return out


def plane_laplace(planes, z, matrix):
    here = planes(z)
    high, low = halves(here)
    along_y = jnp.dot(
        jnp.concatenate([high, low], axis=1),
        jnp.concatenate([matrix, matrix], axis=0),
        preferred_element_type=F32,
    )
    along_x = jnp.dot(
        jnp.concatenate([matrix, matrix], axis=1),
        jnp.concatenate([high, low], axis=0),
        preferred_element_type=F32,
    )
    total = CENTER * here + SCALE * (along_y + along_x)
    for k in range(1, 5):
        total = total + WEIGHTS[k - 1] * (planes(z - k) + planes(z + k))
    return total


def plane_reader(count, low_ref, ref, high_ref):
    def planes(i):
        if i < 0:
            return low_ref[i + 4]
        if i >= count:
            return high_ref[i - count]
        return ref[i]

    return planes


def stencil_matrix(width):
    rows = lax.broadcasted_iota(jnp.int32, (width, width), 0)
    cols = lax.broadcasted_iota(jnp.int32, (width, width), 1)
    return band(jnp.abs(rows - cols)).astype(BF16)


def step_kernel(count, where_ref, strength_ref, now_ref, low_ref, high_ref, prev_ref, vel_ref, born_ref, lap_ref, next_ref, first_ref, last_ref):
    width = now_ref.shape[1]
    matrix = stencil_matrix(width)
    planes = plane_reader(count, low_ref, now_ref, high_ref)
    rows = lax.broadcasted_iota(jnp.int32, (width, width), 0)
    cols = lax.broadcasted_iota(jnp.int32, (width, width), 1)
    hit = (rows == where_ref[1]) & (cols == where_ref[2])
    spot = jnp.where(hit, strength_ref[0], 0.0)
    for z in range(count):
        lap = plane_laplace(planes, z, matrix)
        born = vel_ref[z] * lap
        upcoming = 2.0 * now_ref[z] - prev_ref[z] + born
        upcoming = upcoming + jnp.where(where_ref[0] == z, 1.0, 0.0) * spot
        lap_ref[z] = lap
        born_ref[z] = born
        next_ref[z] = upcoming
        if z < 4:
            first_ref[z] = upcoming
        if z >= count - 4:
            last_ref[z - (count - 4)] = upcoming


def second_kernel(count, strips, wells_ref, next_ref, low_ref, high_ref, born_ref, lap_ref, buf_ref):
    width = next_ref.shape[1]
    matrix = stencil_matrix(width)
    planes = plane_reader(count, low_ref, next_ref, high_ref)
    for z in range(count):
        both = 2.0 * lap_ref[z] + plane_laplace(planes, z, matrix)
        born = born_ref[z]
        for strip in range(strips):
            for half in range(2):
                x = strip * 16 + half * 8
                row = half * count * 8 + z * 8
                buf_ref[strip, row : row + 8, :] = born[x : x + 8]
                buf_ref[strip, 2 * count * 8 + row : 2 * count * 8 + row + 8, :] = both[x : x + 8]
    for strip in range(strips):
        buf_ref[strip, 4 * count * 8 :, :] = wells_ref[...]


def masks_of(wells, width):
    x_row = wells // width
    y_row = wells - x_row * width
    y_ids = lax.broadcasted_iota(jnp.int32, (width, wells.shape[1]), 0)
    distance = jnp.abs(y_ids - y_row)
    spot = jnp.where(distance == 0, 1.0, 0.0).astype(BF16)
    return x_row, spot, band(distance).astype(BF16)


def fill(x_row, spot, side, x, spot_ref, lap_ref, row):
    width = spot.shape[0]
    distance = jnp.abs(x_row - x)
    at = jnp.where(distance == 0, 1.0, 0.0).astype(BF16)
    near = band(distance).astype(BF16)
    spot_ref[row : row + width, :] = spot * at
    lap_ref[row : row + width, :] = spot * near + side * at


def gather_kernel(count, probes, groups, table_ref, wells_ref, vel_ref, buf_ref, *refs):
    n_in = len(groups)
    m_refs = refs[:n_in]
    first_ref, sigma_ref, v_ref, spot_ref, lap_ref, left_ref = refs[n_in:]
    width = buf_ref.shape[2]
    rows = probes * count
    x_row, spot, side = masks_of(wells_ref[...], width)
    first_ref[...] = jnp.zeros_like(first_ref)
    sigma_ref[...] = jnp.zeros_like(sigma_ref)
    v_ref[...] = jnp.zeros_like(v_ref)
    base = 0
    for m_ref, (pieces, half) in zip(m_refs, groups):

        def body(i, carry, m_ref=m_ref, base=base, half=half):
            strip = table_ref[base + i]
            for x in range(8):
                fill(x_row, spot, side, strip * 16 + half * 8 + x, spot_ref, lap_ref, x * width)
                m = m_ref[i, pl.ds(x, rows, stride=8), :]
                born = buf_ref[strip, pl.ds(half * count * 8 + x, count, stride=8), :]
                both = buf_ref[strip, pl.ds((2 + half) * count * 8 + x, count, stride=8), :]
                vel = vel_ref[pl.ds(strip * 16 + half * 8 + x, count, stride=width), :]
                centre = (both + CENTER * born) * (1.0 / SCALE)
                first = m * jnp.concatenate([born] * probes, axis=0)
                other = m * jnp.concatenate([centre] * probes, axis=0)
                columns = slice(x * width, (x + 1) * width)
                for j, value in enumerate((first, other)):
                    high, low = halves(value)
                    left_ref[2 * j * rows : (2 * j + 1) * rows, columns] = high
                    left_ref[(2 * j + 1) * rows : (2 * j + 2) * rows, columns] = low
                high, low = halves(vel)
                left_ref[4 * rows : 4 * rows + count, columns] = high
                left_ref[4 * rows + count :, columns] = low
            out = jnp.dot(left_ref[...], spot_ref[...], preferred_element_type=F32)
            lap = jnp.dot(left_ref[: 2 * rows, :], lap_ref[...], preferred_element_type=F32)
            first_ref[...] += out[:rows] + out[rows : 2 * rows]
            sigma_ref[...] += (out[2 * rows : 3 * rows] + out[3 * rows : 4 * rows]) + (lap[:rows] + lap[rows:])
            v_ref[...] += out[4 * rows : 4 * rows + count] + out[4 * rows + count :]
            return carry

        lax.fori_loop(0, pieces, body, 0)
        base += pieces


def image_kernel(count, probes, shots, strip_ref, well_ref, late_ref, buf_ref, m_ref, out_ref, spot_ref, lap_ref, left_ref, side_ref):
    width = m_ref.shape[1]
    rows = probes * count
    shot = pl.program_id(0)
    n_wells = late_ref.shape[2]

    @pl.when(shot == 0)
    def _():
        out_ref[...] = jnp.zeros_like(out_ref)

    x_row, spot, side = masks_of(well_ref[0], width)
    for p in range(probes):
        top = p * (count + 8)
        here = late_ref[0, top + 4 : top + 4 + count, :]
        along_z = CENTER * here
        for k in range(1, 5):
            along_z = along_z + WEIGHTS[k - 1] * (
                late_ref[0, top + 4 - k : top + 4 - k + count, :] + late_ref[0, top + 4 + k : top + 4 + k + count, :]
            )
        for j, value in enumerate((along_z, here)):
            high, low = halves(value)
            left_ref[2 * j * rows + p * count : 2 * j * rows + (p + 1) * count, :] = high
            left_ref[(2 * j + 1) * rows + p * count : (2 * j + 1) * rows + (p + 1) * count, :] = low
        high, low = halves(SCALE * here)
        side_ref[p * count : (p + 1) * count, :] = high
        side_ref[rows + p * count : rows + (p + 1) * count, :] = low
    left_ref[4 * rows :, :] = jnp.ones((count, n_wells), BF16)
    contract = (((1,), (1,)), ((), ()))
    for half in range(2):
        for pair in range(4):
            for j in range(2):
                x = half * 8 + pair * 2 + j
                fill(x_row, spot, side, strip_ref[0] * 16 + x, spot_ref, lap_ref, j * width)
            out = lax.dot_general(left_ref[...], spot_ref[...], contract, preferred_element_type=F32)
            lap = lax.dot_general(side_ref[...], lap_ref[...], contract, preferred_element_type=F32)
            field = (out[:rows] + out[rows : 2 * rows]) + (lap[:rows] + lap[rows:])
            late = out[2 * rows : 3 * rows] + out[3 * rows : 4 * rows]
            hits = out[4 * rows :]
            for j in range(2):
                x = pair * 2 + j
                columns = slice(j * width, (j + 1) * width)
                born = buf_ref[0, pl.ds(half * count * 8 + x, count, stride=8), :]
                both = buf_ref[0, pl.ds((2 + half) * count * 8 + x, count, stride=8), :]
                seen = hits[:, columns] * born
                m_rows = pl.ds(half * 8 + x, rows, stride=16)
                tile = lambda value: jnp.concatenate([value] * probes, axis=0)
                out_ref[m_rows, :] += (
                    tile(born) * (field[:, columns] + tile(seen) * m_ref[m_rows, :]) + tile(both) * late[:, columns]
                )

    @pl.when(shot == shots - 1)
    def _():
        out_ref[...] = out_ref[...] * (1.0 / shots)


VMEM = pl.BlockSpec(memory_space=pltpu.VMEM)
SMEM = pl.BlockSpec(memory_space=pltpu.SMEM)


def spread(low_layers, high_layers, axis="space"):
    count = lax.axis_size(axis)
    forward = [(i, i + 1) for i in range(count - 1)]
    backward = [(i + 1, i) for i in range(count - 1)]
    return lax.ppermute(high_layers, axis, forward), lax.ppermute(low_layers, axis, backward)


def per_device(wave_prev, wave_now, velocity, probe_panel, source_depth, source_column, source_strength, receiver_wells):
    count, width = wave_now.shape[1], wave_now.shape[2]
    probes = probe_panel.shape[0]
    strips = lax.axis_size("shot")
    n_wells = receiver_wells.shape[1]
    rows = probes * count
    me = lax.axis_index("shot")
    params = pltpu.CompilerParams(vmem_limit_bytes=60 * 1024 * 1024)

    rounds = strips // 2
    swap = [(i, i ^ 1) for i in range(strips)]

    def ring(shift):
        return [(i, (i + 2 * shift) % strips) for i in range(strips)]

    piece = (probes, count, 8, width)
    part_a, part_b = probe_panel[:, :, :8], probe_panel[:, :, 8:]
    now_low, now_high = spread(wave_now[0, :4], wave_now[0, count - 4 :])
    a_swapped = lax.ppermute(part_a, "shot", swap)
    b_ring = [lax.ppermute(part_b, "shot", ring(s)) for s in range(1, rounds)]
    a_pair = jnp.stack([part_a, a_swapped])
    b_all = jnp.stack([part_b] + b_ring)
    b_other = lax.ppermute(b_all, "shot", swap)
    a_ring = [lax.ppermute(a_pair, "shot", ring(s)) for s in range(1, rounds)]

    first_row = lax.axis_index("space") * count
    where = jnp.stack([source_depth[0] - first_row, source_column[0] // width, source_column[0] % width]).astype(jnp.int32)
    plane = jax.ShapeDtypeStruct((count, width, width), F32)
    edge = jax.ShapeDtypeStruct((4, width, width), F32)
    born, lap, upcoming, up_first, up_last = pl.pallas_call(
        functools.partial(step_kernel, count),
        out_shape=(plane, plane, plane, edge, edge),
        in_specs=[SMEM, SMEM] + [VMEM] * 5,
        out_specs=(VMEM,) * 5,
        compiler_params=params,
        name="step_kernel",
    )(where, source_strength, wave_now[0], now_low, now_high, wave_prev[0], velocity)
    up_low, up_high = spread(up_first, up_last)

    well_rows = n_wells // width
    packed_wells = jnp.pad(receiver_wells.reshape(well_rows, width).astype(F32), ((0, 8 - well_rows), (0, 0)))
    buf_rows = 4 * count * 8 + 8
    buf = pl.pallas_call(
        functools.partial(second_kernel, count, strips),
        out_shape=jax.ShapeDtypeStruct((strips, buf_rows, width), F32),
        in_specs=[VMEM] * 6,
        out_specs=VMEM,
        compiler_params=params,
        name="second_kernel",
    )(packed_wells, upcoming, up_low, up_high, born, lap)
    shared = lax.all_to_all(buf, "shot", 0, 0, tiled=True)

    compact = jax.ShapeDtypeStruct((rows, n_wells), F32)

    def gather(parts, halves_of, strip_ids):
        parts = [part.reshape(-1, rows * 8, width) for part in parts]
        groups = tuple((part.shape[0], half) for part, half in zip(parts, halves_of))
        return pl.pallas_call(
            functools.partial(gather_kernel, count, probes, groups),
            out_shape=(compact, compact, jax.ShapeDtypeStruct((count, n_wells), F32)),
            in_specs=[SMEM] + [VMEM] * (3 + len(parts)),
            out_specs=(VMEM,) * 3,
            scratch_shapes=[
                pltpu.VMEM((8 * width, n_wells), BF16),
                pltpu.VMEM((8 * width, n_wells), BF16),
                pltpu.VMEM((4 * rows + 2 * count, 8 * width), BF16),
            ],
            compiler_params=params,
            name="gather_kernel",
        )(jnp.stack(strip_ids).astype(jnp.int32), receiver_wells, velocity.reshape(count * width, width), buf, *parts)

    other = me ^ 1

    def came_from(start, shift):
        return (start - 2 * shift + strips) % strips

    own = gather([a_pair, b_all], (0, 1), [me, other] + [came_from(me, s) for s in range(rounds)])
    far_ids = [i for s in range(1, rounds) for i in (came_from(me, s), came_from(other, s))]
    far = gather(a_ring + [b_other], (0,) * len(a_ring) + (1,), far_ids + [came_from(other, s) for s in range(rounds)])
    first, sigma, vel = [x + y for x, y in zip(own, far)]

    first = first.reshape(probes, count, n_wells)
    low, high = spread(first[:, :4], first[:, count - 4 :])
    wide = jnp.concatenate([low, first, high], axis=1)
    sigma = SCALE * sigma.reshape(probes, count, n_wells)
    for k in range(1, 5):
        sigma = sigma + WEIGHTS[k - 1] * (wide[:, 4 - k : 4 - k + count] + wide[:, 4 + k : 4 + k + count])
    late = (vel * vel)[None] * sigma
    low, high = spread(late[:, :4], late[:, count - 4 :])
    late = jnp.concatenate([low, late, high], axis=1).reshape(probes * (count + 8), n_wells)
    late_all = lax.all_to_all(jnp.broadcast_to(late[None], (strips,) + late.shape), "shot", 0, 0, tiled=True)

    wells_all = shared[:, 4 * count * 8 : 4 * count * 8 + well_rows].astype(jnp.int32).reshape(strips, 1, n_wells)
    image = pl.pallas_call(
        functools.partial(image_kernel, count, probes, strips),
        out_shape=jax.ShapeDtypeStruct((rows * 16, width), F32),
        grid=(strips,),
        in_specs=[
            SMEM,
            pl.BlockSpec((1, 1, n_wells), lambda s: (s, 0, 0)),
            pl.BlockSpec((1, probes * (count + 8), n_wells), lambda s: (s, 0, 0)),
            pl.BlockSpec((1, buf_rows, width), lambda s: (s, 0, 0)),
            pl.BlockSpec((rows * 16, width), lambda s: (0, 0)),
        ],
        out_specs=pl.BlockSpec((rows * 16, width), lambda s: (0, 0)),
        scratch_shapes=[
            pltpu.VMEM((2 * width, n_wells), BF16),
            pltpu.VMEM((2 * width, n_wells), BF16),
            pltpu.VMEM((4 * rows + count, n_wells), BF16),
            pltpu.VMEM((2 * rows, n_wells), BF16),
        ],
        compiler_params=params,
        name="image_kernel",
    )(me.reshape(1).astype(jnp.int32), wells_all, late_all, shared, probe_panel.reshape(rows * 16, width))
    return image.reshape(probe_panel.shape)


def solution(mesh):
    return jax.shard_map(
        per_device,
        mesh=mesh,
        in_specs=(
            P("shot", "space", None, None),
            P("shot", "space", None, None),
            P("space", None, None),
            P(None, "space", "shot", None),
            P("shot"),
            P("shot"),
            P("shot"),
            P("shot", None),
        ),
        out_specs=P(None, "space", "shot", None),
        check_vma=False,
    )
```

```python
import functools

import jax
import jax.numpy as jnp
from jax import lax
from jax.experimental import pallas as pl
from jax.experimental.pallas import tpu as pltpu
from jax.sharding import PartitionSpec as P


CENTER = 3.0 * (-205.0 / 72.0)
WEIGHTS = (8.0 / 5.0, -1.0 / 5.0, 8.0 / 315.0, -1.0 / 560.0)
SCALE = WEIGHTS[0]
RATIOS = tuple(w / SCALE for w in WEIGHTS)
F32 = jnp.float32
BF16 = jnp.bfloat16


def halves(value):
    high = value.astype(BF16)
    low = (value - high.astype(F32)).astype(BF16)
    return high, low


def band(distance):
    out = jnp.zeros(distance.shape, F32)
    for k in range(1, 5):
        out = jnp.where(distance == k, RATIOS[k - 1], out)
    return out


def plane_laplace(planes, z, matrix):
    here = planes(z)
    high, low = halves(here)
    along_y = jnp.dot(
        jnp.concatenate([high, low], axis=1),
        jnp.concatenate([matrix, matrix], axis=0),
        preferred_element_type=F32,
    )
    along_x = jnp.dot(
        jnp.concatenate([matrix, matrix], axis=1),
        jnp.concatenate([high, low], axis=0),
        preferred_element_type=F32,
    )
    total = CENTER * here + SCALE * (along_y + along_x)
    for k in range(1, 5):
        total = total + WEIGHTS[k - 1] * (planes(z - k) + planes(z + k))
    return total


def plane_reader(count, low_ref, ref, high_ref):
    def planes(i):
        if i < 0:
            return low_ref[i + 4]
        if i >= count:
            return high_ref[i - count]
        return ref[i]

    return planes


def stencil_matrix(width):
    rows = lax.broadcasted_iota(jnp.int32, (width, width), 0)
    cols = lax.broadcasted_iota(jnp.int32, (width, width), 1)
    return band(jnp.abs(rows - cols)).astype(BF16)


def step_kernel(count, slab_ref, depth_ref, column_ref, strength_ref, now_ref, low_ref, high_ref, prev_ref, vel_ref, born_ref, lap_ref, next_ref, first_ref, last_ref):
    width = now_ref.shape[1]
    matrix = stencil_matrix(width)
    planes = plane_reader(count, low_ref, now_ref, high_ref)
    rows = lax.broadcasted_iota(jnp.int32, (width, width), 0)
    cols = lax.broadcasted_iota(jnp.int32, (width, width), 1)
    hit = (rows * width + cols) == column_ref[0]
    source_z = depth_ref[0] - slab_ref[0] * count
    spot = jnp.where(hit, strength_ref[0], 0.0)
    for z in range(count):
        lap = plane_laplace(planes, z, matrix)
        born = vel_ref[z] * lap
        upcoming = 2.0 * now_ref[z] - prev_ref[z] + born
        upcoming = upcoming + jnp.where(source_z == z, 1.0, 0.0) * spot
        lap_ref[z] = lap
        born_ref[z] = born
        next_ref[z] = upcoming
        if z < 4:
            first_ref[z] = upcoming
        if z >= count - 4:
            last_ref[z - (count - 4)] = upcoming


def second_kernel(count, strips, wells_ref, next_ref, low_ref, high_ref, born_ref, lap_ref, buf_ref):
    width = next_ref.shape[1]
    matrix = stencil_matrix(width)
    planes = plane_reader(count, low_ref, next_ref, high_ref)
    for z in range(count):
        both = 2.0 * lap_ref[z] + plane_laplace(planes, z, matrix)
        born = born_ref[z]
        for strip in range(strips):
            for half in range(2):
                x = strip * 16 + half * 8
                row = half * count * 8 + z * 8
                buf_ref[strip, row : row + 8, :] = born[x : x + 8]
                buf_ref[strip, 2 * count * 8 + row : 2 * count * 8 + row + 8, :] = both[x : x + 8]
    n_rows = wells_ref.shape[1] // width
    for strip in range(strips):
        for i in range(n_rows):
            row = 4 * count * 8 + i
            buf_ref[strip, row : row + 1, :] = wells_ref[:, i * width : (i + 1) * width].astype(F32)
        buf_ref[strip, 4 * count * 8 + n_rows :, :] = jnp.zeros((buf_ref.shape[1] - 4 * count * 8 - n_rows, width), F32)


def masks_of(wells, width):
    x_row = wells // width
    y_row = wells - x_row * width
    y_ids = lax.broadcasted_iota(jnp.int32, (width, wells.shape[1]), 0)
    spot = jnp.where(y_ids == y_row, 1.0, 0.0).astype(BF16)
    side = jnp.dot(stencil_matrix(width), spot, preferred_element_type=F32).astype(BF16)
    return x_row, spot, side


def fill(x_row, spot, side, x, spot_ref, lap_ref, row):
    width = spot.shape[0]
    distance = jnp.abs(x_row - x)
    at = jnp.where(distance == 0, 1.0, 0.0).astype(BF16)
    near = band(distance).astype(BF16)
    spot_ref[row : row + width, :] = spot * at
    lap_ref[row : row + width, :] = spot * near + side * at


def strip_of(me, rounds, plan, i):
    shift = plan[1] + plan[2] * i
    flip = plan[3] + plan[4] * i
    row = me // 2
    return lax.rem(row - shift + rounds, rounds) * 2 + ((me - 2 * row) ^ flip)


def gather_kernel(count, probes, rounds, plans, counts, started, me_ref, wells_ref, vel_ref, buf_ref, *refs):
    n_in = len(plans)
    m_refs = refs[:n_in]
    refs = refs[n_in:]
    if started:
        start_refs, refs = refs[:3], refs[3:]
    first_ref, sigma_ref, v_ref = refs[:3]
    spot_ref, lap_ref, left_ref = refs[-3:]
    width = buf_ref.shape[2]
    rows = probes * count
    x_row, spot, side = masks_of(wells_ref[...], width)
    if started:
        for ref, start_ref in zip((first_ref, sigma_ref, v_ref), start_refs):
            ref[...] = start_ref[...]
    else:
        for ref in (first_ref, sigma_ref, v_ref):
            ref[...] = jnp.zeros_like(ref)
    for m_ref, plan, pieces in zip(m_refs, plans, counts):

        def body(i, carry, m_ref=m_ref, plan=plan):
            half = plan[0]
            strip = strip_of(me_ref[0], rounds, plan, i)
            for x in range(8):
                fill(x_row, spot, side, strip * 16 + half * 8 + x, spot_ref, lap_ref, x * width)
                m = m_ref[i, pl.ds(x, rows, stride=8), :]
                born = buf_ref[strip, pl.ds(half * count * 8 + x, count, stride=8), :]
                both = buf_ref[strip, pl.ds((2 + half) * count * 8 + x, count, stride=8), :]
                vel = vel_ref[pl.ds(strip * 16 + half * 8 + x, count, stride=width), :]
                centre = (both + CENTER * born) * (1.0 / SCALE)
                first = m * jnp.concatenate([born] * probes, axis=0)
                other = m * jnp.concatenate([centre] * probes, axis=0)
                columns = slice(x * width, (x + 1) * width)
                for j, value in enumerate((first, other)):
                    high, low = halves(value)
                    left_ref[2 * j * rows : (2 * j + 1) * rows, columns] = high
                    left_ref[(2 * j + 1) * rows : (2 * j + 2) * rows, columns] = low
                high, low = halves(vel)
                left_ref[4 * rows : 4 * rows + count, columns] = high
                left_ref[4 * rows + count :, columns] = low
            out = jnp.dot(left_ref[...], spot_ref[...], preferred_element_type=F32)
            lap = jnp.dot(left_ref[: 2 * rows, :], lap_ref[...], preferred_element_type=F32)
            first_ref[...] += out[:rows] + out[rows : 2 * rows]
            sigma_ref[...] += (out[2 * rows : 3 * rows] + out[3 * rows : 4 * rows]) + (lap[:rows] + lap[rows:])
            v_ref[...] += out[4 * rows : 4 * rows + count] + out[4 * rows + count :]
            return carry

        lax.fori_loop(0, pieces, body, 0)
    if started:
        for send_ref, top in ((refs[3], False), (refs[4], True)):
            for p in range(probes):
                z = p * count + (count - 8 if top else 0)
                send_ref[8 * p : 8 * p + 8, :] = first_ref[z : z + 8, :]
                z = p * count + (count - 4 if top else 0)
                send_ref[8 * probes + 4 * p : 8 * probes + 4 * p + 4, :] = sigma_ref[z : z + 4, :]
            z = count - 4 if top else 0
            send_ref[12 * probes : 12 * probes + 4, :] = v_ref[z : z + 4, :]
            send_ref[12 * probes + 4 :, :] = jnp.zeros((4, send_ref.shape[1]), F32)


def late_kernel(count, probes, first_ref, sigma_ref, v_ref, low_ref, high_ref, late_ref, f_ref, s_ref, w_ref):
    deep = count + 8
    top = 12 * probes
    w_ref[:4, :] = low_ref[top : top + 4, :]
    w_ref[4 : 4 + count, :] = v_ref[...]
    w_ref[4 + count :, :] = high_ref[top : top + 4, :]
    w = w_ref[...]
    w = w * w
    for p in range(probes):
        f_ref[:8, :] = low_ref[8 * p : 8 * p + 8, :]
        f_ref[8 : 8 + count, :] = first_ref[p * count : (p + 1) * count, :]
        f_ref[8 + count :, :] = high_ref[8 * p : 8 * p + 8, :]
        z = 8 * probes + 4 * p
        s_ref[:4, :] = low_ref[z : z + 4, :]
        s_ref[4 : 4 + count, :] = sigma_ref[p * count : (p + 1) * count, :]
        s_ref[4 + count :, :] = high_ref[z : z + 4, :]
        sigma = SCALE * s_ref[...]
        for k in range(1, 5):
            sigma = sigma + WEIGHTS[k - 1] * (f_ref[4 - k : 4 - k + deep, :] + f_ref[4 + k : 4 + k + deep, :])
        late_ref[p * deep : (p + 1) * deep, :] = w * sigma


def image_kernel(count, probes, flips, scale, started, me_ref, buf_ref, m_ref, *refs):
    n = len(flips)
    late_refs, refs = refs[:n], refs[n:]
    if started:
        start_ref, refs = refs[0], refs[1:]
    out_ref, late_ref, spot_ref, lap_ref, left_ref, side_ref = refs
    width = m_ref.shape[1]
    rows = probes * count
    step = pl.program_id(0)
    n_wells = late_ref.shape[1]

    @pl.when(step == 0)
    def _():
        out_ref[...] = start_ref[...] if started else jnp.zeros_like(out_ref)

    for i in range(n):

        @pl.when(step == i)
        def _(i=i):
            late_ref[...] = late_refs[i][...]

    top = 4 * count * 8
    wells = jnp.concatenate([buf_ref[0, top + i : top + i + 1, :] for i in range(n_wells // width)], axis=1)
    x_row, spot, side = masks_of(wells.astype(jnp.int32), width)
    for p in range(probes):
        top = p * (count + 8)
        here = late_ref[top + 4 : top + 4 + count, :]
        along_z = CENTER * here
        for k in range(1, 5):
            along_z = along_z + WEIGHTS[k - 1] * (
                late_ref[top + 4 - k : top + 4 - k + count, :] + late_ref[top + 4 + k : top + 4 + k + count, :]
            )
        for j, value in enumerate((along_z, here)):
            high, low = halves(value)
            left_ref[2 * j * rows + p * count : 2 * j * rows + (p + 1) * count, :] = high
            left_ref[(2 * j + 1) * rows + p * count : (2 * j + 1) * rows + (p + 1) * count, :] = low
        high, low = halves(SCALE * here)
        side_ref[p * count : (p + 1) * count, :] = high
        side_ref[rows + p * count : rows + (p + 1) * count, :] = low
    left_ref[4 * rows :, :] = jnp.ones((count, n_wells), BF16)
    contract = (((1,), (1,)), ((), ()))
    for half in range(2):
        for pair in range(4):
            slot = pair % 2
            for j in range(2):
                x = half * 8 + pair * 2 + j
                fill(x_row, spot, side, me_ref[0] * 16 + x, spot_ref.at[slot], lap_ref.at[slot], j * width)
            out = lax.dot_general(left_ref[...], spot_ref[slot], contract, preferred_element_type=F32)
            lap = lax.dot_general(side_ref[...], lap_ref[slot], contract, preferred_element_type=F32)
            field = (out[:rows] + out[rows : 2 * rows]) + (lap[:rows] + lap[rows:])
            late = out[2 * rows : 3 * rows] + out[3 * rows : 4 * rows]
            hits = out[4 * rows :]
            for j in range(2):
                x = pair * 2 + j
                columns = slice(j * width, (j + 1) * width)
                born = buf_ref[0, pl.ds(half * count * 8 + x, count, stride=8), :]
                both = buf_ref[0, pl.ds((2 + half) * count * 8 + x, count, stride=8), :]
                seen = hits[:, columns] * born
                m_rows = pl.ds(half * 8 + x, rows, stride=16)
                tile = lambda value: jnp.concatenate([value] * probes, axis=0)
                out_ref[m_rows, :] += (
                    tile(born) * (field[:, columns] + tile(seen) * m_ref[m_rows, :]) + tile(both) * late[:, columns]
                )

    if scale != 1.0:

        @pl.when(step == n - 1)
        def _():
            out_ref[...] = out_ref[...] * scale


VMEM = pl.BlockSpec(memory_space=pltpu.VMEM)
SMEM = pl.BlockSpec(memory_space=pltpu.SMEM)


def spread(low_layers, high_layers, axis="space"):
    count = lax.axis_size(axis)
    forward = [(i, i + 1) for i in range(count - 1)]
    backward = [(i + 1, i) for i in range(count - 1)]
    return lax.ppermute(high_layers, axis, forward), lax.ppermute(low_layers, axis, backward)


def slab(wave_prev, wave_now, velocity, probe_panel, source_depth, source_column, source_strength, receiver_wells):
    count, width = wave_now.shape[1], wave_now.shape[2]
    probes = probe_panel.shape[0]
    strips = lax.axis_size("shot")
    n_wells = receiver_wells.shape[1]
    rows = probes * count
    me = lax.axis_index("shot").reshape(1).astype(jnp.int32)
    params = pltpu.CompilerParams(vmem_limit_bytes=60 * 1024 * 1024)

    rounds = strips // 2
    swap = [(i, i ^ 1) for i in range(strips)]

    def sent(value, pairs):
        return lax.ppermute(value, "shot", pairs)

    def ring(shift):
        return [(i, (i + 2 * shift) % strips) for i in range(strips)]

    part_a, part_b = probe_panel[:, :, :8], probe_panel[:, :, 8:]
    now_low, now_high = spread(wave_now[0, :4], wave_now[0, count - 4 :])
    a_swapped = sent(part_a, swap)
    b_ring = [sent(part_b, ring(s)) for s in range(1, rounds)]
    a_pair = jnp.stack([part_a, a_swapped])
    b_all = jnp.stack([part_b] + b_ring)
    a_ring = [sent(a_pair, ring(s)) for s in range(1, rounds)]
    b_other = sent(b_all, swap)

    slab_id = lax.axis_index("space").reshape(1).astype(jnp.int32)
    plane = jax.ShapeDtypeStruct((count, width, width), F32)
    edge = jax.ShapeDtypeStruct((4, width, width), F32)
    born, lap, upcoming, up_first, up_last = pl.pallas_call(
        functools.partial(step_kernel, count),
        out_shape=(plane, plane, plane, edge, edge),
        in_specs=[SMEM] * 4 + [VMEM] * 5,
        out_specs=(VMEM,) * 5,
        compiler_params=params,
        name="step_kernel",
    )(slab_id, source_depth, source_column, source_strength, wave_now[0], now_low, now_high, wave_prev[0], velocity)
    up_low, up_high = spread(up_first, up_last)

    buf_rows = 4 * count * 8 + 8
    buf = pl.pallas_call(
        functools.partial(second_kernel, count, strips),
        out_shape=jax.ShapeDtypeStruct((strips, buf_rows, width), F32),
        in_specs=[VMEM] * 6,
        out_specs=VMEM,
        compiler_params=params,
        name="second_kernel",
    )(receiver_wells, upcoming, up_low, up_high, born, lap)
    shared = lax.all_to_all(buf, "shot", 0, 0, tiled=True)

    compact = jax.ShapeDtypeStruct((rows, n_wells), F32)
    compact_v = jax.ShapeDtypeStruct((count, n_wells), F32)
    edge_rows = 12 * probes + 8

    def gather(parts, plans, start=()):
        parts = [part.reshape(-1, rows * 8, width) for part in parts]
        counts = tuple(part.shape[0] for part in parts)
        out_shape = (compact, compact, compact_v)
        if start:
            out_shape += (jax.ShapeDtypeStruct((edge_rows, n_wells), F32),) * 2
        return pl.pallas_call(
            functools.partial(gather_kernel, count, probes, rounds, plans, counts, bool(start)),
            out_shape=out_shape,
            in_specs=[SMEM] + [VMEM] * (3 + len(parts) + len(start)),
            out_specs=(VMEM,) * len(out_shape),
            scratch_shapes=[
                pltpu.VMEM((8 * width, n_wells), BF16),
                pltpu.VMEM((8 * width, n_wells), BF16),
                pltpu.VMEM((4 * rows + 2 * count, 8 * width), BF16),
            ],
            compiler_params=params,
        )(me, receiver_wells, velocity.reshape(count * width, width), buf, *parts, *start)

    own_plans = ((0, 0, 0, 0, 0), (0, 0, 0, 1, 0)) + tuple((1, s, 0, 0, 0) for s in range(rounds))
    own = gather([part_a, a_swapped, part_b] + b_ring, own_plans)
    far_plans = tuple((0, s, 0, 0, 1) for s in range(1, rounds)) + ((1, 0, 1, 1, 0),)
    first, sigma, vel, send_low, send_high = gather(a_ring + [b_other], far_plans, own)
    low, high = spread(send_low, send_high)
    deep = count + 8
    late = pl.pallas_call(
        functools.partial(late_kernel, count, probes),
        out_shape=jax.ShapeDtypeStruct((probes * deep, n_wells), F32),
        in_specs=[VMEM] * 5,
        out_specs=VMEM,
        scratch_shapes=[
            pltpu.VMEM((count + 16, n_wells), F32),
            pltpu.VMEM((deep, n_wells), F32),
            pltpu.VMEM((deep, n_wells), F32),
        ],
        compiler_params=params,
        name="late_kernel",
    )(first, sigma, vel, low, high)

    late_from = {0: late}
    for flip in NEAR + FAR:
        late_from[flip] = sent(late, [(i, i ^ flip) for i in range(strips)])
    panel = probe_panel.reshape(rows * 16, width)

    def image(source, flips, scale, start=()):
        whole = pl.BlockSpec((rows * 16, width), lambda s, me: (0, 0))

        def shot_block(s, me):
            flip = flips[-1]
            for i in range(len(flips) - 2, -1, -1):
                flip = jnp.where(s == i, flips[i], flip)
            return (me[0] ^ flip, 0, 0)

        return pl.pallas_call(
            functools.partial(image_kernel, count, probes, flips, scale, bool(start)),
            out_shape=jax.ShapeDtypeStruct((rows * 16, width), F32),
            grid_spec=pltpu.PrefetchScalarGridSpec(
                num_scalar_prefetch=1,
                grid=(len(flips),),
                in_specs=[pl.BlockSpec((1, buf_rows, width), shot_block), whole]
                + [pl.BlockSpec((probes * deep, n_wells), lambda s, me: (0, 0))] * len(flips)
                + [whole] * len(start),
                out_specs=whole,
                scratch_shapes=[
                    pltpu.VMEM((probes * deep, n_wells), F32),
                    pltpu.VMEM((2, 2 * width, n_wells), BF16),
                    pltpu.VMEM((2, 2 * width, n_wells), BF16),
                    pltpu.VMEM((4 * rows + count, n_wells), BF16),
                    pltpu.VMEM((2 * rows, n_wells), BF16),
                ],
            ),
            compiler_params=params,
        )(me, source, panel, *[late_from[flip] for flip in flips], *start)

    total = image(buf, (0,), 1.0)
    total = image(shared, NEAR, 1.0, (total,))
    total = image(shared, FAR, 1.0 / strips, (total,))
    return total.reshape(probe_panel.shape)


NEAR = (1, 2, 6)
FAR = (3, 7, 4, 5)


def solution(mesh):
    return jax.shard_map(
        slab,
        mesh=mesh,
        in_specs=(
            P("shot", "space", None, None),
            P("shot", "space", None, None),
            P("space", None, None),
            P(None, "space", "shot", None),
            P("shot"),
            P("shot"),
            P("shot"),
            P("shot", None),
        ),
        out_specs=P(None, "space", "shot", None),
        check_vma=False,
    )
```

```python
import functools

import jax
import jax.numpy as jnp
from jax import lax
from jax.experimental import pallas as pl
from jax.experimental.pallas import tpu as pltpu
from jax.sharding import PartitionSpec as P


CENTER = 3.0 * (-205.0 / 72.0)
WEIGHTS = (8.0 / 5.0, -1.0 / 5.0, 8.0 / 315.0, -1.0 / 560.0)
SCALE = WEIGHTS[0]
RATIOS = tuple(w / SCALE for w in WEIGHTS)
F32 = jnp.float32
BF16 = jnp.bfloat16


def halves(value):
    high = value.astype(BF16)
    low = (value - high.astype(F32)).astype(BF16)
    return high, low


def band(distance):
    out = jnp.zeros(distance.shape, F32)
    for k in range(1, 5):
        out = jnp.where(distance == k, RATIOS[k - 1], out)
    return out


def plane_laplace(planes, z, matrix):
    here = planes(z)
    high, low = halves(here)
    along_y = jnp.dot(
        jnp.concatenate([high, low], axis=1),
        jnp.concatenate([matrix, matrix], axis=0),
        preferred_element_type=F32,
    )
    along_x = jnp.dot(
        jnp.concatenate([matrix, matrix], axis=1),
        jnp.concatenate([high, low], axis=0),
        preferred_element_type=F32,
    )
    total = CENTER * here + SCALE * (along_y + along_x)
    for k in range(1, 5):
        total = total + WEIGHTS[k - 1] * (planes(z - k) + planes(z + k))
    return total


def plane_reader(count, low_ref, ref, high_ref):
    def planes(i):
        if i < 0:
            return low_ref[i + 4]
        if i >= count:
            return high_ref[i - count]
        return ref[i]

    return planes


def stencil_matrix(width):
    rows = lax.broadcasted_iota(jnp.int32, (width, width), 0)
    cols = lax.broadcasted_iota(jnp.int32, (width, width), 1)
    return band(jnp.abs(rows - cols)).astype(BF16)


def step_kernel(count, slab_ref, depth_ref, column_ref, strength_ref, now_ref, low_ref, high_ref, prev_ref, vel_ref, born_ref, lap_ref, next_ref, first_ref, last_ref):
    width = now_ref.shape[1]
    matrix = stencil_matrix(width)
    planes = plane_reader(count, low_ref, now_ref, high_ref)
    rows = lax.broadcasted_iota(jnp.int32, (width, width), 0)
    cols = lax.broadcasted_iota(jnp.int32, (width, width), 1)
    hit = (rows * width + cols) == column_ref[0]
    source_z = depth_ref[0] - slab_ref[0] * count
    spot = jnp.where(hit, strength_ref[0], 0.0)
    for z in range(count):
        lap = plane_laplace(planes, z, matrix)
        born = vel_ref[z] * lap
        upcoming = 2.0 * now_ref[z] - prev_ref[z] + born
        upcoming = upcoming + jnp.where(source_z == z, 1.0, 0.0) * spot
        lap_ref[z] = lap
        born_ref[z] = born
        next_ref[z] = upcoming
        if z < 4:
            first_ref[z] = upcoming
        if z >= count - 4:
            last_ref[z - (count - 4)] = upcoming


def second_kernel(count, strips, wells_ref, next_ref, low_ref, high_ref, born_ref, lap_ref, buf_ref):
    width = next_ref.shape[1]
    matrix = stencil_matrix(width)
    planes = plane_reader(count, low_ref, next_ref, high_ref)
    for z in range(count):
        both = 2.0 * lap_ref[z] + plane_laplace(planes, z, matrix)
        born = born_ref[z]
        for strip in range(strips):
            for half in range(2):
                x = strip * 16 + half * 8
                row = half * count * 8 + z * 8
                buf_ref[strip, row : row + 8, :] = born[x : x + 8]
                buf_ref[strip, 2 * count * 8 + row : 2 * count * 8 + row + 8, :] = both[x : x + 8]
    n_rows = wells_ref.shape[1] // width
    for strip in range(strips):
        for i in range(n_rows):
            row = 4 * count * 8 + i
            buf_ref[strip, row : row + 1, :] = wells_ref[:, i * width : (i + 1) * width].astype(F32)
        buf_ref[strip, 4 * count * 8 + n_rows :, :] = jnp.zeros((buf_ref.shape[1] - 4 * count * 8 - n_rows, width), F32)


def masks_of(wells, width, matrix):
    x_row = wells // width
    y_row = wells - x_row * width
    y_ids = lax.broadcasted_iota(jnp.int32, (width, wells.shape[1]), 0)
    spot = jnp.where(y_ids == y_row, 1.0, 0.0).astype(BF16)
    side = jnp.dot(matrix, spot, preferred_element_type=F32).astype(BF16)
    return x_row, spot, side


def rows_of(x_row, base, count):
    ids = base + lax.broadcasted_iota(jnp.int32, (count, x_row.shape[1]), 0)
    distance = jnp.abs(x_row - ids)
    return jnp.where(distance == 0, 1.0, 0.0), band(distance)


def fill(rows, spot, side, x, spot_ref, lap_ref, row):
    width, n = spot.shape
    at, near = (jnp.broadcast_to(value[x : x + 1], (16, n)).astype(BF16)[None] for value in rows)
    spot = spot.reshape(width // 16, 16, n)
    side = side.reshape(width // 16, 16, n)
    spot_ref[row : row + width, :] = (spot * at).reshape(width, n)
    lap_ref[row : row + width, :] = (spot * near + side * at).reshape(width, n)


def strip_of(me, rounds, plan, i):
    shift = plan[1] + plan[2] * i
    flip = plan[3] + plan[4] * i
    row = me // 2
    return lax.rem(row - shift + rounds, rounds) * 2 + ((me - 2 * row) ^ flip)


def gather_kernel(count, probes, rounds, plans, counts, started, me_ref, wells_ref, vel_ref, buf_ref, *refs):
    n_in = len(plans)
    m_refs = refs[:n_in]
    refs = refs[n_in:]
    if started:
        start_refs, refs = refs[:3], refs[3:]
    first_ref, sigma_ref, v_ref = refs[:3]
    spot_ref, lap_ref, left_ref = refs[-3:]
    width = buf_ref.shape[2]
    rows = probes * count
    x_row, spot, side = masks_of(wells_ref[...], width, stencil_matrix(width))
    if started:
        for ref, start_ref in zip((first_ref, sigma_ref, v_ref), start_refs):
            ref[...] = start_ref[...]
    else:
        for ref in (first_ref, sigma_ref, v_ref):
            ref[...] = jnp.zeros_like(ref)
    for m_ref, plan, pieces in zip(m_refs, plans, counts):

        def body(i, carry, m_ref=m_ref, plan=plan):
            half = plan[0]
            strip = strip_of(me_ref[0], rounds, plan, i)
            x_rows = rows_of(x_row, strip * 16 + half * 8, 8)
            for x in range(8):
                fill(x_rows, spot, side, x, spot_ref, lap_ref, x * width)
                m = m_ref[i, pl.ds(x, rows, stride=8), :]
                born = buf_ref[strip, pl.ds(half * count * 8 + x, count, stride=8), :]
                both = buf_ref[strip, pl.ds((2 + half) * count * 8 + x, count, stride=8), :]
                vel = vel_ref[pl.ds(strip * 16 + half * 8 + x, count, stride=width), :]
                centre = (both + CENTER * born) * (1.0 / SCALE)
                first = m * jnp.concatenate([born] * probes, axis=0)
                other = m * jnp.concatenate([centre] * probes, axis=0)
                columns = slice(x * width, (x + 1) * width)
                for j, value in enumerate((first, other)):
                    high, low = halves(value)
                    left_ref[2 * j * rows : (2 * j + 1) * rows, columns] = high
                    left_ref[(2 * j + 1) * rows : (2 * j + 2) * rows, columns] = low
                high, low = halves(vel)
                left_ref[4 * rows : 4 * rows + count, columns] = high
                left_ref[4 * rows + count :, columns] = low
            out = jnp.dot(left_ref[...], spot_ref[...], preferred_element_type=F32)
            lap = jnp.dot(left_ref[: 2 * rows, :], lap_ref[...], preferred_element_type=F32)
            first_ref[...] += out[:rows] + out[rows : 2 * rows]
            sigma_ref[...] += (out[2 * rows : 3 * rows] + out[3 * rows : 4 * rows]) + (lap[:rows] + lap[rows:])
            v_ref[...] += out[4 * rows : 4 * rows + count] + out[4 * rows + count :]
            return carry

        lax.fori_loop(0, pieces, body, 0)
    if started:
        for send_ref, top in ((refs[3], False), (refs[4], True)):
            for p in range(probes):
                z = p * count + (count - 8 if top else 0)
                send_ref[8 * p : 8 * p + 8, :] = first_ref[z : z + 8, :]
                z = p * count + (count - 4 if top else 0)
                send_ref[8 * probes + 4 * p : 8 * probes + 4 * p + 4, :] = sigma_ref[z : z + 4, :]
            z = count - 4 if top else 0
            send_ref[12 * probes : 12 * probes + 4, :] = v_ref[z : z + 4, :]
            send_ref[12 * probes + 4 :, :] = jnp.zeros((4, send_ref.shape[1]), F32)


def late_kernel(count, probes, first_ref, sigma_ref, v_ref, low_ref, high_ref, late_ref, f_ref, s_ref, w_ref):
    deep = count + 8
    top = 12 * probes
    w_ref[:4, :] = low_ref[top : top + 4, :]
    w_ref[4 : 4 + count, :] = v_ref[...]
    w_ref[4 + count :, :] = high_ref[top : top + 4, :]
    w = w_ref[...]
    w = w * w
    for p in range(probes):
        f_ref[:8, :] = low_ref[8 * p : 8 * p + 8, :]
        f_ref[8 : 8 + count, :] = first_ref[p * count : (p + 1) * count, :]
        f_ref[8 + count :, :] = high_ref[8 * p : 8 * p + 8, :]
        z = 8 * probes + 4 * p
        s_ref[:4, :] = low_ref[z : z + 4, :]
        s_ref[4 : 4 + count, :] = sigma_ref[p * count : (p + 1) * count, :]
        s_ref[4 + count :, :] = high_ref[z : z + 4, :]
        sigma = SCALE * s_ref[...]
        for k in range(1, 5):
            sigma = sigma + WEIGHTS[k - 1] * (f_ref[4 - k : 4 - k + deep, :] + f_ref[4 + k : 4 + k + deep, :])
        late_ref[p * deep : (p + 1) * deep, :] = w * sigma


def image_kernel(count, probes, flips, scale, started, me_ref, buf_ref, m_ref, *refs):
    n = len(flips)
    late_refs, refs = refs[:n], refs[n:]
    if started:
        start_ref, refs = refs[0], refs[1:]
    out_ref, late_ref, spot_ref, lap_ref, left_ref, matrix_ref = refs
    width = m_ref.shape[1]
    rows = probes * count
    step = pl.program_id(0)
    n_wells = late_ref.shape[1]

    @pl.when(step == 0)
    def _():
        out_ref[...] = start_ref[...] if started else jnp.zeros_like(out_ref)
        matrix_ref[...] = stencil_matrix(width)

    for i in range(n):

        @pl.when(step == i)
        def _(i=i):
            late_ref[...] = late_refs[i][...]

    top = 4 * count * 8
    wells = jnp.concatenate([buf_ref[0, top + i : top + i + 1, :] for i in range(n_wells // width)], axis=1)
    x_row, spot, side = masks_of(wells.astype(jnp.int32), width, matrix_ref[...])
    x_rows = rows_of(x_row, me_ref[0] * 16, 16)
    for p in range(probes):
        top = p * (count + 8)
        here = late_ref[top + 4 : top + 4 + count, :]
        along_z = CENTER * here
        for k in range(1, 5):
            along_z = along_z + WEIGHTS[k - 1] * (
                late_ref[top + 4 - k : top + 4 - k + count, :] + late_ref[top + 4 + k : top + 4 + k + count, :]
            )
        for j, value in enumerate((along_z, here)):
            high, low = halves(value)
            left_ref[2 * j * rows + p * count : 2 * j * rows + (p + 1) * count, :] = high
            left_ref[(2 * j + 1) * rows + p * count : (2 * j + 1) * rows + (p + 1) * count, :] = low
    left_ref[4 * rows :, :] = jnp.ones((count, n_wells), BF16)
    contract = (((1,), (1,)), ((), ()))
    for half in range(2):
        for pair in range(4):
            slot = pair % 2
            for j in range(2):
                x = half * 8 + pair * 2 + j
                fill(x_rows, spot, side, x, spot_ref.at[slot], lap_ref.at[slot], j * width)
            out = lax.dot_general(left_ref[...], spot_ref[slot], contract, preferred_element_type=F32)
            lap = lax.dot_general(left_ref[2 * rows : 4 * rows, :], lap_ref[slot], contract, preferred_element_type=F32)
            field = (out[:rows] + out[rows : 2 * rows]) + SCALE * (lap[:rows] + lap[rows:])
            late = out[2 * rows : 3 * rows] + out[3 * rows : 4 * rows]
            hits = out[4 * rows :]
            for j in range(2):
                x = pair * 2 + j
                columns = slice(j * width, (j + 1) * width)
                born = buf_ref[0, pl.ds(half * count * 8 + x, count, stride=8), :]
                both = buf_ref[0, pl.ds((2 + half) * count * 8 + x, count, stride=8), :]
                seen = hits[:, columns] * born
                m_rows = pl.ds(half * 8 + x, rows, stride=16)
                tile = lambda value: jnp.concatenate([value] * probes, axis=0)
                out_ref[m_rows, :] += (
                    tile(born) * (field[:, columns] + tile(seen) * m_ref[m_rows, :]) + tile(both) * late[:, columns]
                )

    if scale != 1.0:

        @pl.when(step == n - 1)
        def _():
            out_ref[...] = out_ref[...] * scale


VMEM = pl.BlockSpec(memory_space=pltpu.VMEM)
SMEM = pl.BlockSpec(memory_space=pltpu.SMEM)


def spread(low_layers, high_layers, axis="space"):
    count = lax.axis_size(axis)
    forward = [(i, i + 1) for i in range(count - 1)]
    backward = [(i + 1, i) for i in range(count - 1)]
    return lax.ppermute(high_layers, axis, forward), lax.ppermute(low_layers, axis, backward)


def slab(wave_prev, wave_now, velocity, probe_panel, source_depth, source_column, source_strength, receiver_wells):
    count, width = wave_now.shape[1], wave_now.shape[2]
    probes = probe_panel.shape[0]
    strips = lax.axis_size("shot")
    n_wells = receiver_wells.shape[1]
    rows = probes * count
    me = lax.axis_index("shot").reshape(1).astype(jnp.int32)
    params = pltpu.CompilerParams(vmem_limit_bytes=32 * 1024 * 1024)
    gather_params = pltpu.CompilerParams(vmem_limit_bytes=32 * 1024 * 1024)
    image_params = pltpu.CompilerParams(vmem_limit_bytes=67043328)

    rounds = strips // 2
    swap = [(i, i ^ 1) for i in range(strips)]

    def sent(value, pairs):
        return lax.ppermute(value, "shot", pairs)

    def ring(shift):
        return [(i, (i + 2 * shift) % strips) for i in range(strips)]

    part_a, part_b = probe_panel[:, :, :8], probe_panel[:, :, 8:]
    now_low, now_high = spread(wave_now[0, :4], wave_now[0, count - 4 :])
    a_swapped = sent(part_a, swap)
    b_ring = [sent(part_b, ring(s)) for s in range(1, rounds)]
    a_pair = jnp.stack([part_a, a_swapped])
    b_all = jnp.stack([part_b] + b_ring)
    a_ring = [sent(a_pair, ring(s)) for s in range(1, rounds)]
    b_other = sent(b_all, swap)

    slab_id = lax.axis_index("space").reshape(1).astype(jnp.int32)
    plane = jax.ShapeDtypeStruct((count, width, width), F32)
    edge = jax.ShapeDtypeStruct((4, width, width), F32)
    born, lap, upcoming, up_first, up_last = pl.pallas_call(
        functools.partial(step_kernel, count),
        out_shape=(plane, plane, plane, edge, edge),
        in_specs=[SMEM] * 4 + [VMEM] * 5,
        out_specs=(VMEM,) * 5,
        compiler_params=params,
        name="step_kernel",
    )(slab_id, source_depth, source_column, source_strength, wave_now[0], now_low, now_high, wave_prev[0], velocity)
    up_low, up_high = spread(up_first, up_last)

    buf_rows = 4 * count * 8 + 8
    buf = pl.pallas_call(
        functools.partial(second_kernel, count, strips),
        out_shape=jax.ShapeDtypeStruct((strips, buf_rows, width), F32),
        in_specs=[VMEM] * 6,
        out_specs=VMEM,
        compiler_params=params,
        name="second_kernel",
    )(receiver_wells, upcoming, up_low, up_high, born, lap)
    shared = lax.all_to_all(buf, "shot", 0, 0, tiled=True)

    compact = jax.ShapeDtypeStruct((rows, n_wells), F32)
    compact_v = jax.ShapeDtypeStruct((count, n_wells), F32)
    edge_rows = 12 * probes + 8

    def gather(parts, plans, start=()):
        parts = [part.reshape(-1, rows * 8, width) for part in parts]
        counts = tuple(part.shape[0] for part in parts)
        out_shape = (compact, compact, compact_v)
        if start:
            out_shape += (jax.ShapeDtypeStruct((edge_rows, n_wells), F32),) * 2
        return pl.pallas_call(
            functools.partial(gather_kernel, count, probes, rounds, plans, counts, bool(start)),
            out_shape=out_shape,
            in_specs=[SMEM] + [VMEM] * (3 + len(parts) + len(start)),
            out_specs=(VMEM,) * len(out_shape),
            scratch_shapes=[
                pltpu.VMEM((8 * width, n_wells), BF16),
                pltpu.VMEM((8 * width, n_wells), BF16),
                pltpu.VMEM((4 * rows + 2 * count, 8 * width), BF16),
            ],
            compiler_params=gather_params,
        )(me, receiver_wells, velocity.reshape(count * width, width), buf, *parts, *start)

    own_plans = ((0, 0, 0, 0, 0), (0, 0, 0, 1, 0)) + tuple((1, s, 0, 0, 0) for s in range(rounds))
    own = gather([part_a, a_swapped, part_b] + b_ring, own_plans)
    far_plans = tuple((0, s, 0, 0, 1) for s in range(1, rounds)) + ((1, 0, 1, 1, 0),)
    first, sigma, vel, send_low, send_high = gather(a_ring + [b_other], far_plans, own)
    low, high = spread(send_low, send_high)
    deep = count + 8
    late = pl.pallas_call(
        functools.partial(late_kernel, count, probes),
        out_shape=jax.ShapeDtypeStruct((probes * deep, n_wells), F32),
        in_specs=[VMEM] * 5,
        out_specs=VMEM,
        scratch_shapes=[
            pltpu.VMEM((count + 16, n_wells), F32),
            pltpu.VMEM((deep, n_wells), F32),
            pltpu.VMEM((deep, n_wells), F32),
        ],
        compiler_params=params,
        name="late_kernel",
    )(first, sigma, vel, low, high)

    late_from = {0: late}
    for flip in NEAR + FAR:
        late_from[flip] = sent(late, [(i, i ^ flip) for i in range(strips)])
    panel = probe_panel.reshape(rows * 16, width)

    def image(source, flips, scale, start=()):
        whole = pl.BlockSpec((rows * 16, width), lambda s, me: (0, 0))

        def shot_block(s, me):
            flip = flips[-1]
            for i in range(len(flips) - 2, -1, -1):
                flip = jnp.where(s == i, flips[i], flip)
            return (me[0] ^ flip, 0, 0)

        return pl.pallas_call(
            functools.partial(image_kernel, count, probes, flips, scale, bool(start)),
            out_shape=jax.ShapeDtypeStruct((rows * 16, width), F32),
            grid_spec=pltpu.PrefetchScalarGridSpec(
                num_scalar_prefetch=1,
                grid=(len(flips),),
                in_specs=[pl.BlockSpec((1, buf_rows, width), shot_block), whole]
                + [pl.BlockSpec((probes * deep, n_wells), lambda s, me: (0, 0))] * len(flips)
                + [whole] * len(start),
                out_specs=whole,
                scratch_shapes=[
                    pltpu.VMEM((probes * deep, n_wells), F32),
                    pltpu.VMEM((2, 2 * width, n_wells), BF16),
                    pltpu.VMEM((2, 2 * width, n_wells), BF16),
                    pltpu.VMEM((4 * rows + count, n_wells), BF16),
                    pltpu.VMEM((width, width), BF16),
                ],
            ),
            compiler_params=image_params,
        )(me, source, panel, *[late_from[flip] for flip in flips], *start)

    total = image(buf, (0,), 1.0)
    total = image(shared, NEAR, 1.0, (total,))
    total = image(shared, FAR, 1.0 / strips, (total,))
    return total.reshape(probe_panel.shape)


NEAR = (1, 2, 6)
FAR = (3, 7, 4, 5)


def solution(mesh):
    return jax.shard_map(
        slab,
        mesh=mesh,
        in_specs=(
            P("shot", "space", None, None),
            P("shot", "space", None, None),
            P("space", None, None),
            P(None, "space", "shot", None),
            P("shot"),
            P("shot"),
            P("shot"),
            P("shot", None),
        ),
        out_specs=P(None, "space", "shot", None),
        check_vma=False,
    )
```

```python
import functools

import jax
import jax.numpy as jnp
from jax import lax
from jax.experimental import pallas as pl
from jax.experimental.pallas import tpu as pltpu
from jax.sharding import PartitionSpec as P


CENTER = 3.0 * (-205.0 / 72.0)
WEIGHTS = (8.0 / 5.0, -1.0 / 5.0, 8.0 / 315.0, -1.0 / 560.0)
SCALE = WEIGHTS[0]
RATIOS = tuple(w / SCALE for w in WEIGHTS)
F32 = jnp.float32
BF16 = jnp.bfloat16


def halves(value):
    high = value.astype(BF16)
    low = (value - high.astype(F32)).astype(BF16)
    return high, low


def band(distance):
    out = jnp.zeros(distance.shape, F32)
    for k in range(1, 5):
        out = jnp.where(distance == k, RATIOS[k - 1], out)
    return out


def plane_laplace(planes, z, matrix):
    here = planes(z)
    high, low = halves(here)
    along_y = jnp.dot(
        jnp.concatenate([high, low], axis=1),
        jnp.concatenate([matrix, matrix], axis=0),
        preferred_element_type=F32,
    )
    along_x = jnp.dot(
        jnp.concatenate([matrix, matrix], axis=1),
        jnp.concatenate([high, low], axis=0),
        preferred_element_type=F32,
    )
    total = CENTER * here + SCALE * (along_y + along_x)
    for k in range(1, 5):
        total = total + WEIGHTS[k - 1] * (planes(z - k) + planes(z + k))
    return total


def plane_reader(count, low_ref, ref, high_ref):
    def planes(i):
        if i < 0:
            return low_ref[i + 4]
        if i >= count:
            return high_ref[i - count]
        return ref[i]

    return planes


def stencil_matrix(width):
    rows = lax.broadcasted_iota(jnp.int32, (width, width), 0)
    cols = lax.broadcasted_iota(jnp.int32, (width, width), 1)
    return band(jnp.abs(rows - cols)).astype(BF16)


def step_kernel(count, slab_ref, depth_ref, column_ref, strength_ref, now_ref, low_ref, high_ref, prev_ref, vel_ref, born_ref, lap_ref, next_ref, first_ref, last_ref):
    width = now_ref.shape[1]
    matrix = stencil_matrix(width)
    planes = plane_reader(count, low_ref, now_ref, high_ref)
    rows = lax.broadcasted_iota(jnp.int32, (width, width), 0)
    cols = lax.broadcasted_iota(jnp.int32, (width, width), 1)
    hit = (rows * width + cols) == column_ref[0]
    source_z = depth_ref[0] - slab_ref[0] * count
    spot = jnp.where(hit, strength_ref[0], 0.0)
    for z in range(count):
        lap = plane_laplace(planes, z, matrix)
        born = vel_ref[z] * lap
        upcoming = 2.0 * now_ref[z] - prev_ref[z] + born
        upcoming = upcoming + jnp.where(source_z == z, 1.0, 0.0) * spot
        lap_ref[z] = lap
        born_ref[z] = born
        next_ref[z] = upcoming
        if z < 4:
            first_ref[z] = upcoming
        if z >= count - 4:
            last_ref[z - (count - 4)] = upcoming


def second_kernel(count, strips, wells_ref, next_ref, low_ref, high_ref, born_ref, lap_ref, buf_ref):
    width = next_ref.shape[1]
    matrix = stencil_matrix(width)
    planes = plane_reader(count, low_ref, next_ref, high_ref)
    for z in range(count):
        both = 2.0 * lap_ref[z] + plane_laplace(planes, z, matrix)
        born = born_ref[z]
        for strip in range(strips):
            for half in range(2):
                x = strip * 16 + half * 8
                row = half * count * 8 + z * 8
                buf_ref[strip, row : row + 8, :] = born[x : x + 8]
                buf_ref[strip, 2 * count * 8 + row : 2 * count * 8 + row + 8, :] = both[x : x + 8]
    n_rows = wells_ref.shape[1] // width
    for strip in range(strips):
        for i in range(n_rows):
            row = 4 * count * 8 + i
            buf_ref[strip, row : row + 1, :] = wells_ref[:, i * width : (i + 1) * width].astype(F32)
        buf_ref[strip, 4 * count * 8 + n_rows :, :] = jnp.zeros((buf_ref.shape[1] - 4 * count * 8 - n_rows, width), F32)


def masks_of(wells, width, matrix):
    x_row = wells // width
    y_row = wells - x_row * width
    y_ids = lax.broadcasted_iota(jnp.int32, (width, wells.shape[1]), 0)
    spot = jnp.where(y_ids == y_row, 1.0, 0.0).astype(BF16)
    side = jnp.dot(matrix, spot, preferred_element_type=F32).astype(BF16)
    return x_row, spot, side


def rows_of(x_row, base, count):
    ids = base + lax.broadcasted_iota(jnp.int32, (count, x_row.shape[1]), 0)
    distance = jnp.abs(x_row - ids)
    return jnp.where(distance == 0, 1.0, 0.0), band(distance)


def fill(rows, spot, side, x, spot_ref, lap_ref, row):
    width, n = spot.shape
    at, near = (jnp.broadcast_to(value[x : x + 1], (16, n)).astype(BF16)[None] for value in rows)
    spot = spot.reshape(width // 16, 16, n)
    side = side.reshape(width // 16, 16, n)
    spot_ref[row : row + width, :] = (spot * at).reshape(width, n)
    lap_ref[row : row + width, :] = (spot * near + side * at).reshape(width, n)


def strip_of(me, rounds, plan, i):
    shift = plan[1] + plan[2] * i
    flip = plan[3] + plan[4] * i
    row = me // 2
    return lax.rem(row - shift + rounds, rounds) * 2 + ((me - 2 * row) ^ flip)


def gather_kernel(count, probes, rounds, plans, counts, started, me_ref, wells_ref, vel_ref, buf_ref, *refs):
    n_in = len(plans)
    m_refs = refs[:n_in]
    refs = refs[n_in:]
    if started:
        start_refs, refs = refs[:3], refs[3:]
    first_ref, sigma_ref, v_ref = refs[:3]
    spot_ref, lap_ref, left_ref = refs[-3:]
    width = buf_ref.shape[2]
    rows = probes * count
    x_row, spot, side = masks_of(wells_ref[...], width, stencil_matrix(width))
    if started:
        for ref, start_ref in zip((first_ref, sigma_ref, v_ref), start_refs):
            ref[...] = start_ref[...]
    else:
        for ref in (first_ref, sigma_ref, v_ref):
            ref[...] = jnp.zeros_like(ref)
    jobs = []
    for m_ref, plan, pieces in zip(m_refs, plans, counts):
        if plan[0] is None:
            jobs += [(m_ref, plan, 1, 0), (m_ref, plan, 1, 1)]
        else:
            jobs += [(m_ref, plan, pieces, plan[0])]
    for m_ref, plan, pieces, half in jobs:

        def body(i, carry, m_ref=m_ref, plan=plan, half=half):
            strip = strip_of(me_ref[0], rounds, plan, i)
            x_rows = rows_of(x_row, strip * 16 + half * 8, 8)
            for x in range(8):
                fill(x_rows, spot, side, x, spot_ref, lap_ref, x * width)
                m = m_ref[0, pl.ds(half * 8 + x, rows, stride=16), :] if plan[0] is None else m_ref[i, pl.ds(x, rows, stride=8), :]
                born = buf_ref[strip, pl.ds(half * count * 8 + x, count, stride=8), :]
                both = buf_ref[strip, pl.ds((2 + half) * count * 8 + x, count, stride=8), :]
                vel = vel_ref[pl.ds(strip * 16 + half * 8 + x, count, stride=width), :]
                centre = (both + CENTER * born) * (1.0 / SCALE)
                first = m * jnp.concatenate([born] * probes, axis=0)
                other = m * jnp.concatenate([centre] * probes, axis=0)
                columns = slice(x * width, (x + 1) * width)
                for j, value in enumerate((first, other)):
                    high, low = halves(value)
                    left_ref[2 * j * rows : (2 * j + 1) * rows, columns] = high
                    left_ref[(2 * j + 1) * rows : (2 * j + 2) * rows, columns] = low
                high, low = halves(vel)
                left_ref[4 * rows : 4 * rows + count, columns] = high
                left_ref[4 * rows + count :, columns] = low
            out = jnp.dot(left_ref[...], spot_ref[...], preferred_element_type=F32)
            lap = jnp.dot(left_ref[: 2 * rows, :], lap_ref[...], preferred_element_type=F32)
            first_ref[...] += out[:rows] + out[rows : 2 * rows]
            sigma_ref[...] += (out[2 * rows : 3 * rows] + out[3 * rows : 4 * rows]) + (lap[:rows] + lap[rows:])
            v_ref[...] += out[4 * rows : 4 * rows + count] + out[4 * rows + count :]
            return carry

        lax.fori_loop(0, pieces, body, 0)
    if started:
        for send_ref, top in ((refs[3], False), (refs[4], True)):
            for p in range(probes):
                z = p * count + (count - 8 if top else 0)
                send_ref[8 * p : 8 * p + 8, :] = first_ref[z : z + 8, :]
                z = p * count + (count - 4 if top else 0)
                send_ref[8 * probes + 4 * p : 8 * probes + 4 * p + 4, :] = sigma_ref[z : z + 4, :]
            z = count - 4 if top else 0
            send_ref[12 * probes : 12 * probes + 4, :] = v_ref[z : z + 4, :]
            send_ref[12 * probes + 4 :, :] = jnp.zeros((4, send_ref.shape[1]), F32)


def late_kernel(count, probes, first_ref, sigma_ref, v_ref, low_ref, high_ref, late_ref, f_ref, s_ref, w_ref):
    deep = count + 8
    top = 12 * probes
    w_ref[:4, :] = low_ref[top : top + 4, :]
    w_ref[4 : 4 + count, :] = v_ref[...]
    w_ref[4 + count :, :] = high_ref[top : top + 4, :]
    w = w_ref[...]
    w = w * w
    for p in range(probes):
        f_ref[:8, :] = low_ref[8 * p : 8 * p + 8, :]
        f_ref[8 : 8 + count, :] = first_ref[p * count : (p + 1) * count, :]
        f_ref[8 + count :, :] = high_ref[8 * p : 8 * p + 8, :]
        z = 8 * probes + 4 * p
        s_ref[:4, :] = low_ref[z : z + 4, :]
        s_ref[4 : 4 + count, :] = sigma_ref[p * count : (p + 1) * count, :]
        s_ref[4 + count :, :] = high_ref[z : z + 4, :]
        sigma = SCALE * s_ref[...]
        for k in range(1, 5):
            sigma = sigma + WEIGHTS[k - 1] * (f_ref[4 - k : 4 - k + deep, :] + f_ref[4 + k : 4 + k + deep, :])
        late_ref[p * deep : (p + 1) * deep, :] = w * sigma


def image_kernel(count, probes, flips, scale, started, me_ref, buf_ref, m_ref, *refs):
    n = len(flips)
    late_refs, refs = refs[:n], refs[n:]
    if started:
        start_ref, refs = refs[0], refs[1:]
    out_ref, late_ref, spot_ref, lap_ref, left_ref, matrix_ref = refs
    width = m_ref.shape[1]
    rows = probes * count
    step = pl.program_id(0)
    n_wells = late_ref.shape[1]

    @pl.when(step == 0)
    def _():
        out_ref[...] = start_ref[...] if started else jnp.zeros_like(out_ref)
        matrix_ref[...] = stencil_matrix(width)

    for i in range(n):

        @pl.when(step == i)
        def _(i=i):
            late_ref[...] = late_refs[i][...]

    top = 4 * count * 8
    wells = jnp.concatenate([buf_ref[0, top + i : top + i + 1, :] for i in range(n_wells // width)], axis=1)
    x_row, spot, side = masks_of(wells.astype(jnp.int32), width, matrix_ref[...])
    x_rows = rows_of(x_row, me_ref[0] * 16, 16)
    for p in range(probes):
        top = p * (count + 8)
        here = late_ref[top + 4 : top + 4 + count, :]
        along_z = CENTER * here
        for k in range(1, 5):
            along_z = along_z + WEIGHTS[k - 1] * (
                late_ref[top + 4 - k : top + 4 - k + count, :] + late_ref[top + 4 + k : top + 4 + k + count, :]
            )
        for j, value in enumerate((along_z, here)):
            high, low = halves(value)
            left_ref[2 * j * rows + p * count : 2 * j * rows + (p + 1) * count, :] = high
            left_ref[(2 * j + 1) * rows + p * count : (2 * j + 1) * rows + (p + 1) * count, :] = low
    left_ref[4 * rows :, :] = jnp.ones((count, n_wells), BF16)
    contract = (((1,), (1,)), ((), ()))
    for half in range(2):
        for pair in range(4):
            slot = pair % 2
            for j in range(2):
                x = half * 8 + pair * 2 + j
                fill(x_rows, spot, side, x, spot_ref.at[slot], lap_ref.at[slot], j * width)
            out = lax.dot_general(left_ref[...], spot_ref[slot], contract, preferred_element_type=F32)
            lap = lax.dot_general(left_ref[2 * rows : 4 * rows, :], lap_ref[slot], contract, preferred_element_type=F32)
            field = (out[:rows] + out[rows : 2 * rows]) + SCALE * (lap[:rows] + lap[rows:])
            late = out[2 * rows : 3 * rows] + out[3 * rows : 4 * rows]
            hits = out[4 * rows :]
            for j in range(2):
                x = pair * 2 + j
                columns = slice(j * width, (j + 1) * width)
                born = buf_ref[0, pl.ds(half * count * 8 + x, count, stride=8), :]
                both = buf_ref[0, pl.ds((2 + half) * count * 8 + x, count, stride=8), :]
                seen = hits[:, columns] * born
                m_rows = pl.ds(half * 8 + x, rows, stride=16)
                tile = lambda value: jnp.concatenate([value] * probes, axis=0)
                out_ref[m_rows, :] += (
                    tile(born) * (field[:, columns] + tile(seen) * m_ref[m_rows, :]) + tile(both) * late[:, columns]
                )

    if scale != 1.0:

        @pl.when(step == n - 1)
        def _():
            out_ref[...] = out_ref[...] * scale


VMEM = pl.BlockSpec(memory_space=pltpu.VMEM)
SMEM = pl.BlockSpec(memory_space=pltpu.SMEM)


def spread(low_layers, high_layers, axis="space"):
    count = lax.axis_size(axis)
    forward = [(i, i + 1) for i in range(count - 1)]
    backward = [(i + 1, i) for i in range(count - 1)]
    return lax.ppermute(high_layers, axis, forward), lax.ppermute(low_layers, axis, backward)


def slab(wave_prev, wave_now, velocity, probe_panel, source_depth, source_column, source_strength, receiver_wells):
    count, width = wave_now.shape[1], wave_now.shape[2]
    probes = probe_panel.shape[0]
    strips = lax.axis_size("shot")
    n_wells = receiver_wells.shape[1]
    rows = probes * count
    me = lax.axis_index("shot").reshape(1).astype(jnp.int32)
    params = pltpu.CompilerParams(vmem_limit_bytes=52 * 1024 * 1024)
    gather_params = pltpu.CompilerParams(vmem_limit_bytes=40 * 1024 * 1024)
    image_params = pltpu.CompilerParams(vmem_limit_bytes=67043328)

    rounds = strips // 2
    swap = [(i, i ^ 1) for i in range(strips)]

    def sent(value, pairs):
        return lax.ppermute(value, "shot", pairs)

    def ring(shift):
        return [(i, (i + 2 * shift) % strips) for i in range(strips)]

    now_low, now_high = spread(wave_now[0, :4], wave_now[0, count - 4 :])
    swapped = sent(probe_panel, swap)
    part_b = probe_panel[:, :, 8:]
    b_ring = [sent(part_b, ring(s)) for s in range(1, rounds)]
    a_pair = jnp.stack([probe_panel[:, :, :8], swapped[:, :, :8]])
    a_ring = [sent(a_pair, ring(s)) for s in range(1, rounds)]
    b_other = sent(jnp.stack(b_ring), swap)

    slab_id = lax.axis_index("space").reshape(1).astype(jnp.int32)
    plane = jax.ShapeDtypeStruct((count, width, width), F32)
    edge = jax.ShapeDtypeStruct((4, width, width), F32)
    born, lap, upcoming, up_first, up_last = pl.pallas_call(
        functools.partial(step_kernel, count),
        out_shape=(plane, plane, plane, edge, edge),
        in_specs=[SMEM] * 4 + [VMEM] * 5,
        out_specs=(VMEM,) * 5,
        compiler_params=params,
        name="step_kernel",
    )(slab_id, source_depth, source_column, source_strength, wave_now[0], now_low, now_high, wave_prev[0], velocity)
    up_low, up_high = spread(up_first, up_last)

    buf_rows = 4 * count * 8 + 8
    buf = pl.pallas_call(
        functools.partial(second_kernel, count, strips),
        out_shape=jax.ShapeDtypeStruct((strips, buf_rows, width), F32),
        in_specs=[VMEM] * 6,
        out_specs=VMEM,
        compiler_params=params,
        name="second_kernel",
    )(receiver_wells, upcoming, up_low, up_high, born, lap)
    shared = lax.all_to_all(buf, "shot", 0, 0, tiled=True)

    compact = jax.ShapeDtypeStruct((rows, n_wells), F32)
    compact_v = jax.ShapeDtypeStruct((count, n_wells), F32)
    edge_rows = 12 * probes + 8

    def gather(parts, plans, start=()):
        parts = [part.reshape(-1, rows * (16 if plan[0] is None else 8), width) for part, plan in zip(parts, plans)]
        counts = tuple(part.shape[0] for part in parts)
        out_shape = (compact, compact, compact_v)
        if start:
            out_shape += (jax.ShapeDtypeStruct((edge_rows, n_wells), F32),) * 2
        return pl.pallas_call(
            functools.partial(gather_kernel, count, probes, rounds, plans, counts, bool(start)),
            out_shape=out_shape,
            in_specs=[SMEM] + [VMEM] * (3 + len(parts) + len(start)),
            out_specs=(VMEM,) * len(out_shape),
            scratch_shapes=[
                pltpu.VMEM((8 * width, n_wells), BF16),
                pltpu.VMEM((8 * width, n_wells), BF16),
                pltpu.VMEM((4 * rows + 2 * count, 8 * width), BF16),
            ],
            compiler_params=gather_params,
        )(me, receiver_wells, velocity.reshape(count * width, width), buf, *parts, *start)

    own_plans = ((None, 0, 0, 0, 0), (None, 0, 0, 1, 0)) + tuple((1, s, 0, 0, 0) for s in range(1, rounds))
    own = gather([probe_panel, swapped] + b_ring, own_plans)
    far_plans = tuple((0, s, 0, 0, 1) for s in range(1, rounds)) + ((1, 1, 1, 1, 0),)
    first, sigma, vel, send_low, send_high = gather(a_ring + [b_other], far_plans, own)
    low, high = spread(send_low, send_high)
    deep = count + 8
    late = pl.pallas_call(
        functools.partial(late_kernel, count, probes),
        out_shape=jax.ShapeDtypeStruct((probes * deep, n_wells), F32),
        in_specs=[VMEM] * 5,
        out_specs=VMEM,
        scratch_shapes=[
            pltpu.VMEM((count + 16, n_wells), F32),
            pltpu.VMEM((deep, n_wells), F32),
            pltpu.VMEM((deep, n_wells), F32),
        ],
        compiler_params=params,
        name="late_kernel",
    )(first, sigma, vel, low, high)

    late_from = {0: late}
    for flip in NEAR + FAR:
        late_from[flip] = sent(late, [(i, i ^ flip) for i in range(strips)])
    panel = probe_panel.reshape(rows * 16, width)

    def image(source, flips, scale, start=()):
        whole = pl.BlockSpec((rows * 16, width), lambda s, me: (0, 0))

        def shot_block(s, me):
            flip = flips[-1]
            for i in range(len(flips) - 2, -1, -1):
                flip = jnp.where(s == i, flips[i], flip)
            return (me[0] ^ flip, 0, 0)

        return pl.pallas_call(
            functools.partial(image_kernel, count, probes, flips, scale, bool(start)),
            out_shape=jax.ShapeDtypeStruct((rows * 16, width), F32),
            grid_spec=pltpu.PrefetchScalarGridSpec(
                num_scalar_prefetch=1,
                grid=(len(flips),),
                in_specs=[pl.BlockSpec((1, buf_rows, width), shot_block), whole]
                + [pl.BlockSpec((probes * deep, n_wells), lambda s, me: (0, 0))] * len(flips)
                + [whole] * len(start),
                out_specs=whole,
                scratch_shapes=[
                    pltpu.VMEM((probes * deep, n_wells), F32),
                    pltpu.VMEM((2, 2 * width, n_wells), BF16),
                    pltpu.VMEM((2, 2 * width, n_wells), BF16),
                    pltpu.VMEM((4 * rows + count, n_wells), BF16),
                    pltpu.VMEM((width, width), BF16),
                ],
            ),
            compiler_params=image_params,
        )(me, source, panel, *[late_from[flip] for flip in flips], *start)

    total = image(buf, (0,), 1.0)
    total = image(shared, NEAR, 1.0, (total,))
    total = image(shared, FAR, 1.0 / strips, (total,))
    return total.reshape(probe_panel.shape)


NEAR = (1, 2, 6)
FAR = (3, 7, 4, 5)


def solution(mesh):
    return jax.shard_map(
        slab,
        mesh=mesh,
        in_specs=(
            P("shot", "space", None, None),
            P("shot", "space", None, None),
            P("space", None, None),
            P(None, "space", "shot", None),
            P("shot"),
            P("shot"),
            P("shot"),
            P("shot", None),
        ),
        out_specs=P(None, "space", "shot", None),
        check_vma=False,
    )
```

```python
import functools

import jax
import jax.numpy as jnp
from jax import lax
from jax.experimental import pallas as pl
from jax.experimental.pallas import tpu as pltpu
from jax.sharding import PartitionSpec as P


CENTER = 3.0 * (-205.0 / 72.0)
WEIGHTS = (8.0 / 5.0, -1.0 / 5.0, 8.0 / 315.0, -1.0 / 560.0)
SCALE = WEIGHTS[0]
RATIOS = tuple(w / SCALE for w in WEIGHTS)
F32 = jnp.float32
BF16 = jnp.bfloat16


def halves(value):
    high = value.astype(BF16)
    low = (value - high.astype(F32)).astype(BF16)
    return high, low


def band(distance):
    out = jnp.zeros(distance.shape, F32)
    for k in range(1, 5):
        out = jnp.where(distance == k, RATIOS[k - 1], out)
    return out


def plane_laplace(planes, z, matrix):
    here = planes(z)
    high, low = halves(here)
    along_y = jnp.dot(
        jnp.concatenate([high, low], axis=1),
        jnp.concatenate([matrix, matrix], axis=0),
        preferred_element_type=F32,
    )
    along_x = jnp.dot(
        jnp.concatenate([matrix, matrix], axis=1),
        jnp.concatenate([high, low], axis=0),
        preferred_element_type=F32,
    )
    total = CENTER * here + SCALE * (along_y + along_x)
    for k in range(1, 5):
        total = total + WEIGHTS[k - 1] * (planes(z - k) + planes(z + k))
    return total


def plane_reader(count, low_ref, ref, high_ref):
    def planes(i):
        if i < 0:
            return low_ref[i + 4]
        if i >= count:
            return high_ref[i - count]
        return ref[i]

    return planes


def stencil_matrix(width):
    rows = lax.broadcasted_iota(jnp.int32, (width, width), 0)
    cols = lax.broadcasted_iota(jnp.int32, (width, width), 1)
    return band(jnp.abs(rows - cols)).astype(BF16)


def step_kernel(count, slab_ref, depth_ref, column_ref, strength_ref, now_ref, low_ref, high_ref, prev_ref, vel_ref, born_ref, lap_ref, next_ref, first_ref, last_ref):
    width = now_ref.shape[1]
    matrix = stencil_matrix(width)
    planes = plane_reader(count, low_ref, now_ref, high_ref)
    rows = lax.broadcasted_iota(jnp.int32, (width, width), 0)
    cols = lax.broadcasted_iota(jnp.int32, (width, width), 1)
    hit = (rows * width + cols) == column_ref[0]
    source_z = depth_ref[0] - slab_ref[0] * count
    spot = jnp.where(hit, strength_ref[0], 0.0)
    for z in range(count):
        lap = plane_laplace(planes, z, matrix)
        born = vel_ref[z] * lap
        upcoming = 2.0 * now_ref[z] - prev_ref[z] + born
        upcoming = upcoming + jnp.where(source_z == z, 1.0, 0.0) * spot
        lap_ref[z] = lap
        born_ref[z] = born
        next_ref[z] = upcoming
        if z < 4:
            first_ref[z] = upcoming
        if z >= count - 4:
            last_ref[z - (count - 4)] = upcoming


def second_kernel(count, strips, wells_ref, next_ref, low_ref, high_ref, born_ref, lap_ref, buf_ref):
    width = next_ref.shape[1]
    matrix = stencil_matrix(width)
    planes = plane_reader(count, low_ref, next_ref, high_ref)
    for z in range(count):
        both = 2.0 * lap_ref[z] + plane_laplace(planes, z, matrix)
        born = born_ref[z]
        for strip in range(strips):
            for half in range(2):
                x = strip * 16 + half * 8
                row = half * count * 8 + z * 8
                buf_ref[strip, row : row + 8, :] = born[x : x + 8]
                buf_ref[strip, 2 * count * 8 + row : 2 * count * 8 + row + 8, :] = both[x : x + 8]
    n_rows = wells_ref.shape[1] // width
    for strip in range(strips):
        for i in range(n_rows):
            row = 4 * count * 8 + i
            buf_ref[strip, row : row + 1, :] = wells_ref[:, i * width : (i + 1) * width].astype(F32)
        buf_ref[strip, 4 * count * 8 + n_rows :, :] = jnp.zeros((buf_ref.shape[1] - 4 * count * 8 - n_rows, width), F32)


def masks_of(wells, width, matrix):
    x_row = wells // width
    y_row = wells - x_row * width
    y_ids = lax.broadcasted_iota(jnp.int32, (width, wells.shape[1]), 0)
    spot = jnp.where(y_ids == y_row, 1.0, 0.0).astype(BF16)
    side = jnp.dot(matrix, spot, preferred_element_type=F32).astype(BF16)
    return x_row, spot, side


def rows_of(x_row, base, count):
    ids = base + lax.broadcasted_iota(jnp.int32, (count, x_row.shape[1]), 0)
    distance = jnp.abs(x_row - ids)
    return jnp.where(distance == 0, 1.0, 0.0), band(distance)


def fill(rows, spot, side, x, spot_ref, lap_ref, row):
    width, n = spot.shape
    at, near = (jnp.broadcast_to(value[x : x + 1], (16, n)).astype(BF16)[None] for value in rows)
    spot = spot.reshape(width // 16, 16, n)
    side = side.reshape(width // 16, 16, n)
    spot_ref[row : row + width, :] = (spot * at).reshape(width, n)
    lap_ref[row : row + width, :] = (spot * near + side * at).reshape(width, n)


def strip_of(me, rounds, plan, i):
    shift = plan[1] + plan[2] * i
    flip = plan[3] + plan[4] * i
    row = me // 2
    return lax.rem(row - shift + rounds, rounds) * 2 + ((me - 2 * row) ^ flip)


def gather_kernel(count, probes, rounds, plans, counts, started, ended, me_ref, wells_ref, vel_ref, buf_ref, *refs):
    n_in = len(plans)
    m_refs = refs[:n_in]
    refs = refs[n_in:]
    if started:
        start_refs, refs = refs[:3], refs[3:]
    first_ref, sigma_ref, v_ref = refs[:3]
    spot_ref, lap_ref, left_ref = refs[-3:]
    width = buf_ref.shape[2]
    rows = probes * count
    x_row, spot, side = masks_of(wells_ref[...], width, stencil_matrix(width))
    if started:
        for ref, start_ref in zip((first_ref, sigma_ref, v_ref), start_refs):
            ref[...] = start_ref[...]
    else:
        for ref in (first_ref, sigma_ref, v_ref):
            ref[...] = jnp.zeros_like(ref)
    jobs = []
    for m_ref, plan, pieces in zip(m_refs, plans, counts):
        if plan[0] is None:
            jobs += [(m_ref, plan, 1, 0), (m_ref, plan, 1, 1)]
        else:
            jobs += [(m_ref, plan, pieces, plan[0])]
    for m_ref, plan, pieces, half in jobs:

        def body(i, carry, m_ref=m_ref, plan=plan, half=half):
            strip = strip_of(me_ref[0], rounds, plan, i)
            x_rows = rows_of(x_row, strip * 16 + half * 8, 8)
            for x in range(8):
                fill(x_rows, spot, side, x, spot_ref, lap_ref, x * width)
                m = m_ref[0, pl.ds(half * 8 + x, rows, stride=16), :] if plan[0] is None else m_ref[i, pl.ds(x, rows, stride=8), :]
                born = buf_ref[strip, pl.ds(half * count * 8 + x, count, stride=8), :]
                both = buf_ref[strip, pl.ds((2 + half) * count * 8 + x, count, stride=8), :]
                vel = vel_ref[pl.ds(strip * 16 + half * 8 + x, count, stride=width), :]
                centre = (both + CENTER * born) * (1.0 / SCALE)
                first = m * jnp.concatenate([born] * probes, axis=0)
                other = m * jnp.concatenate([centre] * probes, axis=0)
                columns = slice(x * width, (x + 1) * width)
                for j, value in enumerate((first, other)):
                    high, low = halves(value)
                    left_ref[2 * j * rows : (2 * j + 1) * rows, columns] = high
                    left_ref[(2 * j + 1) * rows : (2 * j + 2) * rows, columns] = low
                high, low = halves(vel)
                left_ref[4 * rows : 4 * rows + count, columns] = high
                left_ref[4 * rows + count :, columns] = low
            out = jnp.dot(left_ref[...], spot_ref[...], preferred_element_type=F32)
            lap = jnp.dot(left_ref[: 2 * rows, :], lap_ref[...], preferred_element_type=F32)
            first_ref[...] += out[:rows] + out[rows : 2 * rows]
            sigma_ref[...] += (out[2 * rows : 3 * rows] + out[3 * rows : 4 * rows]) + (lap[:rows] + lap[rows:])
            v_ref[...] += out[4 * rows : 4 * rows + count] + out[4 * rows + count :]
            return carry

        lax.fori_loop(0, pieces, body, 0)
    if ended:
        for send_ref, top in ((refs[3], False), (refs[4], True)):
            for p in range(probes):
                z = p * count + (count - 8 if top else 0)
                send_ref[8 * p : 8 * p + 8, :] = first_ref[z : z + 8, :]
                z = p * count + (count - 4 if top else 0)
                send_ref[8 * probes + 4 * p : 8 * probes + 4 * p + 4, :] = sigma_ref[z : z + 4, :]
            z = count - 4 if top else 0
            send_ref[12 * probes : 12 * probes + 4, :] = v_ref[z : z + 4, :]
            send_ref[12 * probes + 4 :, :] = jnp.zeros((4, send_ref.shape[1]), F32)


def late_kernel(count, probes, first_ref, sigma_ref, v_ref, low_ref, high_ref, late_ref, f_ref, s_ref, w_ref):
    deep = count + 8
    top = 12 * probes
    w_ref[:4, :] = low_ref[top : top + 4, :]
    w_ref[4 : 4 + count, :] = v_ref[...]
    w_ref[4 + count :, :] = high_ref[top : top + 4, :]
    w = w_ref[...]
    w = w * w
    for p in range(probes):
        f_ref[:8, :] = low_ref[8 * p : 8 * p + 8, :]
        f_ref[8 : 8 + count, :] = first_ref[p * count : (p + 1) * count, :]
        f_ref[8 + count :, :] = high_ref[8 * p : 8 * p + 8, :]
        z = 8 * probes + 4 * p
        s_ref[:4, :] = low_ref[z : z + 4, :]
        s_ref[4 : 4 + count, :] = sigma_ref[p * count : (p + 1) * count, :]
        s_ref[4 + count :, :] = high_ref[z : z + 4, :]
        sigma = SCALE * s_ref[...]
        for k in range(1, 5):
            sigma = sigma + WEIGHTS[k - 1] * (f_ref[4 - k : 4 - k + deep, :] + f_ref[4 + k : 4 + k + deep, :])
        late_ref[p * deep : (p + 1) * deep, :] = w * sigma


def image_kernel(count, probes, flips, scale, started, me_ref, buf_ref, m_ref, *refs):
    n = len(flips)
    late_refs, refs = refs[:n], refs[n:]
    if started:
        start_ref, refs = refs[0], refs[1:]
    out_ref, late_ref, spot_ref, lap_ref, left_ref, matrix_ref = refs
    width = m_ref.shape[1]
    rows = probes * count
    step = pl.program_id(0)
    n_wells = late_ref.shape[1]

    @pl.when(step == 0)
    def _():
        out_ref[...] = start_ref[...] if started else jnp.zeros_like(out_ref)
        matrix_ref[...] = stencil_matrix(width)

    for i in range(n):

        @pl.when(step == i)
        def _(i=i):
            late_ref[...] = late_refs[i][...]

    top = 4 * count * 8
    wells = jnp.concatenate([buf_ref[0, top + i : top + i + 1, :] for i in range(n_wells // width)], axis=1)
    x_row, spot, side = masks_of(wells.astype(jnp.int32), width, matrix_ref[...])
    x_rows = rows_of(x_row, me_ref[0] * 16, 16)
    for p in range(probes):
        top = p * (count + 8)
        here = late_ref[top + 4 : top + 4 + count, :]
        along_z = CENTER * here
        for k in range(1, 5):
            along_z = along_z + WEIGHTS[k - 1] * (
                late_ref[top + 4 - k : top + 4 - k + count, :] + late_ref[top + 4 + k : top + 4 + k + count, :]
            )
        for j, value in enumerate((along_z, here)):
            high, low = halves(value)
            left_ref[2 * j * rows + p * count : 2 * j * rows + (p + 1) * count, :] = high
            left_ref[(2 * j + 1) * rows + p * count : (2 * j + 1) * rows + (p + 1) * count, :] = low
    left_ref[4 * rows :, :] = jnp.ones((count, n_wells), BF16)
    contract = (((1,), (1,)), ((), ()))
    for half in range(2):
        for pair in range(4):
            slot = pair % 2
            for j in range(2):
                x = half * 8 + pair * 2 + j
                fill(x_rows, spot, side, x, spot_ref.at[slot], lap_ref.at[slot], j * width)
            out = lax.dot_general(left_ref[...], spot_ref[slot], contract, preferred_element_type=F32)
            lap = lax.dot_general(left_ref[2 * rows : 4 * rows, :], lap_ref[slot], contract, preferred_element_type=F32)
            field = (out[:rows] + out[rows : 2 * rows]) + SCALE * (lap[:rows] + lap[rows:])
            late = out[2 * rows : 3 * rows] + out[3 * rows : 4 * rows]
            hits = out[4 * rows :]
            for j in range(2):
                x = pair * 2 + j
                columns = slice(j * width, (j + 1) * width)
                born = buf_ref[0, pl.ds(half * count * 8 + x, count, stride=8), :]
                both = buf_ref[0, pl.ds((2 + half) * count * 8 + x, count, stride=8), :]
                seen = hits[:, columns] * born
                m_rows = pl.ds(half * 8 + x, rows, stride=16)
                tile = lambda value: jnp.concatenate([value] * probes, axis=0)
                out_ref[m_rows, :] += (
                    tile(born) * (field[:, columns] + tile(seen) * m_ref[m_rows, :]) + tile(both) * late[:, columns]
                )

    if scale != 1.0:

        @pl.when(step == n - 1)
        def _():
            out_ref[...] = out_ref[...] * scale


VMEM = pl.BlockSpec(memory_space=pltpu.VMEM)
SMEM = pl.BlockSpec(memory_space=pltpu.SMEM)


def spread(low_layers, high_layers, axis="space"):
    count = lax.axis_size(axis)
    forward = [(i, i + 1) for i in range(count - 1)]
    backward = [(i + 1, i) for i in range(count - 1)]
    return lax.ppermute(high_layers, axis, forward), lax.ppermute(low_layers, axis, backward)


def slab(wave_prev, wave_now, velocity, probe_panel, source_depth, source_column, source_strength, receiver_wells):
    count, width = wave_now.shape[1], wave_now.shape[2]
    probes = probe_panel.shape[0]
    strips = lax.axis_size("shot")
    n_wells = receiver_wells.shape[1]
    rows = probes * count
    me = lax.axis_index("shot").reshape(1).astype(jnp.int32)
    params = pltpu.CompilerParams(vmem_limit_bytes=48 * 1024 * 1024)
    gather_params = pltpu.CompilerParams(vmem_limit_bytes=40 * 1024 * 1024)
    image_params = pltpu.CompilerParams(vmem_limit_bytes=67043328)

    rounds = strips // 2
    swap = [(i, i ^ 1) for i in range(strips)]

    def sent(value, pairs):
        return lax.ppermute(value, "shot", pairs)

    def ring(shift):
        return [(i, (i + 2 * shift) % strips) for i in range(strips)]

    now_low, now_high = spread(wave_now[0, :4], wave_now[0, count - 4 :])
    swapped = sent(probe_panel, swap)
    part_b = probe_panel[:, :, 8:]
    b_ring = [sent(part_b, ring(s)) for s in range(1, rounds)]
    a_pair = jnp.stack([probe_panel[:, :, :8], swapped[:, :, :8]])
    a_ring = [sent(a_pair, ring(s)) for s in range(1, rounds)]
    b_stack = jnp.stack(b_ring)
    b_other = sent(b_stack, swap)

    slab_id = lax.axis_index("space").reshape(1).astype(jnp.int32)
    plane = jax.ShapeDtypeStruct((count, width, width), F32)
    edge = jax.ShapeDtypeStruct((4, width, width), F32)
    born, lap, upcoming, up_first, up_last = pl.pallas_call(
        functools.partial(step_kernel, count),
        out_shape=(plane, plane, plane, edge, edge),
        in_specs=[SMEM] * 4 + [VMEM] * 5,
        out_specs=(VMEM,) * 5,
        compiler_params=params,
        name="step_kernel",
    )(slab_id, source_depth, source_column, source_strength, wave_now[0], now_low, now_high, wave_prev[0], velocity)
    up_low, up_high = spread(up_first, up_last)

    buf_rows = 4 * count * 8 + 8
    buf = pl.pallas_call(
        functools.partial(second_kernel, count, strips),
        out_shape=jax.ShapeDtypeStruct((strips, buf_rows, width), F32),
        in_specs=[VMEM] * 6,
        out_specs=VMEM,
        compiler_params=params,
        name="second_kernel",
    )(receiver_wells, upcoming, up_low, up_high, born, lap)
    shared = lax.all_to_all(buf, "shot", 0, 0, tiled=True)

    compact = jax.ShapeDtypeStruct((rows, n_wells), F32)
    compact_v = jax.ShapeDtypeStruct((count, n_wells), F32)
    edge_rows = 12 * probes + 8

    def gather(parts, plans, start=(), ended=False):
        parts = [part.reshape(-1, rows * (16 if plan[0] is None else 8), width) for part, plan in zip(parts, plans)]
        counts = tuple(part.shape[0] for part in parts)
        out_shape = (compact, compact, compact_v)
        if ended:
            out_shape += (jax.ShapeDtypeStruct((edge_rows, n_wells), F32),) * 2
        return pl.pallas_call(
            functools.partial(gather_kernel, count, probes, rounds, plans, counts, bool(start), ended),
            out_shape=out_shape,
            in_specs=[SMEM] + [VMEM] * (3 + len(parts) + len(start)),
            out_specs=(VMEM,) * len(out_shape),
            scratch_shapes=[
                pltpu.VMEM((8 * width, n_wells), BF16),
                pltpu.VMEM((8 * width, n_wells), BF16),
                pltpu.VMEM((4 * rows + 2 * count, 8 * width), BF16),
            ],
            compiler_params=gather_params,
        )(me, receiver_wells, velocity.reshape(count * width, width), buf, *parts, *start)

    own_plans = ((None, 0, 0, 0, 0), (None, 0, 0, 1, 0)) + tuple((1, s, 0, 0, 0) for s in range(1, rounds))
    own = gather([probe_panel, swapped] + b_ring, own_plans)
    first_ring, rest = a_ring[0], a_ring[1:]
    most = gather([first_ring, b_other], ((0, 1, 0, 0, 1), (1, 1, 1, 1, 0)), own)
    last_plans = tuple((0, s, 0, 0, 1) for s in range(2, rounds))
    first, sigma, vel, send_low, send_high = gather(rest, last_plans, most, True)
    low, high = spread(send_low, send_high)
    deep = count + 8
    late = pl.pallas_call(
        functools.partial(late_kernel, count, probes),
        out_shape=jax.ShapeDtypeStruct((probes * deep, n_wells), F32),
        in_specs=[VMEM] * 5,
        out_specs=VMEM,
        scratch_shapes=[
            pltpu.VMEM((count + 16, n_wells), F32),
            pltpu.VMEM((deep, n_wells), F32),
            pltpu.VMEM((deep, n_wells), F32),
        ],
        compiler_params=params,
        name="late_kernel",
    )(first, sigma, vel, low, high)

    late_from = {0: late}
    for flip in NEAR + FAR:
        late_from[flip] = sent(late, [(i, i ^ flip) for i in range(strips)])
    panel = probe_panel.reshape(rows * 16, width)

    def image(source, flips, scale, start=()):
        whole = pl.BlockSpec((rows * 16, width), lambda s, me: (0, 0))

        def shot_block(s, me):
            flip = flips[-1]
            for i in range(len(flips) - 2, -1, -1):
                flip = jnp.where(s == i, flips[i], flip)
            return (me[0] ^ flip, 0, 0)

        return pl.pallas_call(
            functools.partial(image_kernel, count, probes, flips, scale, bool(start)),
            out_shape=jax.ShapeDtypeStruct((rows * 16, width), F32),
            grid_spec=pltpu.PrefetchScalarGridSpec(
                num_scalar_prefetch=1,
                grid=(len(flips),),
                in_specs=[pl.BlockSpec((1, buf_rows, width), shot_block), whole]
                + [pl.BlockSpec((probes * deep, n_wells), lambda s, me: (0, 0))] * len(flips)
                + [whole] * len(start),
                out_specs=whole,
                scratch_shapes=[
                    pltpu.VMEM((probes * deep, n_wells), F32),
                    pltpu.VMEM((2, 2 * width, n_wells), BF16),
                    pltpu.VMEM((2, 2 * width, n_wells), BF16),
                    pltpu.VMEM((4 * rows + count, n_wells), BF16),
                    pltpu.VMEM((width, width), BF16),
                ],
            ),
            compiler_params=image_params,
        )(me, source, panel, *[late_from[flip] for flip in flips], *start)

    total = image(buf, (0,), 1.0)
    total = image(shared, NEAR, 1.0, (total,))
    total = image(shared, FAR, 1.0 / strips, (total,))
    return total.reshape(probe_panel.shape)


NEAR = (1, 2, 6)
FAR = (3, 7, 4, 5)


def solution(mesh):
    return jax.shard_map(
        slab,
        mesh=mesh,
        in_specs=(
            P("shot", "space", None, None),
            P("shot", "space", None, None),
            P("space", None, None),
            P(None, "space", "shot", None),
            P("shot"),
            P("shot"),
            P("shot"),
            P("shot", None),
        ),
        out_specs=P(None, "space", "shot", None),
        check_vma=False,
    )
```

```python
import functools

import jax
import jax.numpy as jnp
from jax import lax
from jax.experimental import pallas as pl
from jax.experimental.pallas import tpu as pltpu
from jax.sharding import PartitionSpec as P


CENTER = 3.0 * (-205.0 / 72.0)
WEIGHTS = (8.0 / 5.0, -1.0 / 5.0, 8.0 / 315.0, -1.0 / 560.0)
SCALE = WEIGHTS[0]
RATIOS = tuple(w / SCALE for w in WEIGHTS)
F32 = jnp.float32
BF16 = jnp.bfloat16


def halves(value):
    high = value.astype(BF16)
    low = (value - high.astype(F32)).astype(BF16)
    return high, low


def band(distance):
    out = jnp.zeros(distance.shape, F32)
    for k in range(1, 5):
        out = jnp.where(distance == k, RATIOS[k - 1], out)
    return out


def plane_laplace(planes, z, matrix):
    here = planes(z)
    high, low = halves(here)
    along_y = jnp.dot(
        jnp.concatenate([high, low], axis=1),
        jnp.concatenate([matrix, matrix], axis=0),
        preferred_element_type=F32,
    )
    along_x = jnp.dot(
        jnp.concatenate([matrix, matrix], axis=1),
        jnp.concatenate([high, low], axis=0),
        preferred_element_type=F32,
    )
    total = CENTER * here + SCALE * (along_y + along_x)
    for k in range(1, 5):
        total = total + WEIGHTS[k - 1] * (planes(z - k) + planes(z + k))
    return total


def plane_reader(count, low_ref, ref, high_ref):
    def planes(i):
        if i < 0:
            return low_ref[i + 4]
        if i >= count:
            return high_ref[i - count]
        return ref[i]

    return planes


def stencil_matrix(width):
    rows = lax.broadcasted_iota(jnp.int32, (width, width), 0)
    cols = lax.broadcasted_iota(jnp.int32, (width, width), 1)
    return band(jnp.abs(rows - cols)).astype(BF16)


def step_kernel(count, slab_ref, depth_ref, column_ref, strength_ref, now_ref, low_ref, high_ref, prev_ref, vel_ref, born_ref, lap_ref, next_ref, first_ref, last_ref):
    width = now_ref.shape[1]
    matrix = stencil_matrix(width)
    planes = plane_reader(count, low_ref, now_ref, high_ref)
    rows = lax.broadcasted_iota(jnp.int32, (width, width), 0)
    cols = lax.broadcasted_iota(jnp.int32, (width, width), 1)
    hit = (rows * width + cols) == column_ref[0]
    source_z = depth_ref[0] - slab_ref[0] * count
    spot = jnp.where(hit, strength_ref[0], 0.0)
    for z in range(count):
        lap = plane_laplace(planes, z, matrix)
        born = vel_ref[z] * lap
        upcoming = 2.0 * now_ref[z] - prev_ref[z] + born
        upcoming = upcoming + jnp.where(source_z == z, 1.0, 0.0) * spot
        lap_ref[z] = lap
        born_ref[z] = born
        next_ref[z] = upcoming
        if z < 4:
            first_ref[z] = upcoming
        if z >= count - 4:
            last_ref[z - (count - 4)] = upcoming


def second_kernel(count, strips, wells_ref, next_ref, low_ref, high_ref, born_ref, lap_ref, buf_ref):
    width = next_ref.shape[1]
    matrix = stencil_matrix(width)
    planes = plane_reader(count, low_ref, next_ref, high_ref)
    for z in range(count):
        both = 2.0 * lap_ref[z] + plane_laplace(planes, z, matrix)
        born = born_ref[z]
        for strip in range(strips):
            for half in range(2):
                x = strip * 16 + half * 8
                row = half * count * 8 + z * 8
                buf_ref[strip, row : row + 8, :] = born[x : x + 8]
                buf_ref[strip, 2 * count * 8 + row : 2 * count * 8 + row + 8, :] = both[x : x + 8]
    n_rows = wells_ref.shape[1] // width
    for strip in range(strips):
        for i in range(n_rows):
            row = 4 * count * 8 + i
            buf_ref[strip, row : row + 1, :] = wells_ref[:, i * width : (i + 1) * width].astype(F32)
        buf_ref[strip, 4 * count * 8 + n_rows :, :] = jnp.zeros((buf_ref.shape[1] - 4 * count * 8 - n_rows, width), F32)


def masks_of(wells, width, matrix):
    x_row = wells // width
    y_row = wells - x_row * width
    y_ids = lax.broadcasted_iota(jnp.int32, (width, wells.shape[1]), 0)
    spot = jnp.where(y_ids == y_row, 1.0, 0.0).astype(BF16)
    side = jnp.dot(matrix, spot, preferred_element_type=F32).astype(BF16)
    return x_row, spot, side


def rows_of(x_row, base, count):
    ids = base + lax.broadcasted_iota(jnp.int32, (count, x_row.shape[1]), 0)
    distance = jnp.abs(x_row - ids)
    return jnp.where(distance == 0, 1.0, 0.0), band(distance)


def fill(rows, spot, side, x, spot_ref, lap_ref, row):
    width, n = spot.shape
    at, near = (jnp.broadcast_to(value[x : x + 1], (16, n)).astype(BF16)[None] for value in rows)
    spot = spot.reshape(width // 16, 16, n)
    side = side.reshape(width // 16, 16, n)
    spot_ref[row : row + width, :] = (spot * at).reshape(width, n)
    lap_ref[row : row + width, :] = (spot * near + side * at).reshape(width, n)


def strip_of(me, rounds, plan, i):
    shift = plan[1] + plan[2] * i
    flip = plan[3] + plan[4] * i
    row = me // 2
    return lax.rem(row - shift + rounds, rounds) * 2 + ((me - 2 * row) ^ flip)


def gather_kernel(count, probes, rounds, plans, counts, started, ended, me_ref, wells_ref, vel_ref, buf_ref, *refs):
    n_in = len(plans)
    m_refs = refs[:n_in]
    refs = refs[n_in:]
    if started:
        start_refs, refs = refs[:3], refs[3:]
    first_ref, sigma_ref, v_ref = refs[:3]
    spot_ref, lap_ref, left_ref = refs[-3:]
    width = buf_ref.shape[2]
    rows = probes * count
    x_row, spot, side = masks_of(wells_ref[...], width, stencil_matrix(width))
    if started:
        for ref, start_ref in zip((first_ref, sigma_ref, v_ref), start_refs):
            ref[...] = start_ref[...]
    else:
        for ref in (first_ref, sigma_ref, v_ref):
            ref[...] = jnp.zeros_like(ref)
    jobs = []
    for m_ref, plan, pieces in zip(m_refs, plans, counts):
        if plan[0] is None:
            jobs += [(m_ref, plan, 1, 0), (m_ref, plan, 1, 1)]
        else:
            jobs += [(m_ref, plan, pieces, plan[0])]
    for m_ref, plan, pieces, half in jobs:

        def body(i, carry, m_ref=m_ref, plan=plan, half=half):
            strip = strip_of(me_ref[0], rounds, plan, i)
            x_rows = rows_of(x_row, strip * 16 + half * 8, 8)
            for x in range(8):
                fill(x_rows, spot, side, x, spot_ref, lap_ref, x * width)
                m = m_ref[0, pl.ds(half * 8 + x, rows, stride=16), :] if plan[0] is None else m_ref[i, pl.ds(x, rows, stride=8), :]
                born = buf_ref[strip, pl.ds(half * count * 8 + x, count, stride=8), :]
                both = buf_ref[strip, pl.ds((2 + half) * count * 8 + x, count, stride=8), :]
                vel = vel_ref[pl.ds(strip * 16 + half * 8 + x, count, stride=width), :]
                centre = (both + CENTER * born) * (1.0 / SCALE)
                first = m * jnp.concatenate([born] * probes, axis=0)
                other = m * jnp.concatenate([centre] * probes, axis=0)
                columns = slice(x * width, (x + 1) * width)
                for j, value in enumerate((first, other)):
                    high, low = halves(value)
                    left_ref[2 * j * rows : (2 * j + 1) * rows, columns] = high
                    left_ref[(2 * j + 1) * rows : (2 * j + 2) * rows, columns] = low
                high, low = halves(vel)
                left_ref[4 * rows : 4 * rows + count, columns] = high
                left_ref[4 * rows + count :, columns] = low
            out = jnp.dot(left_ref[...], spot_ref[...], preferred_element_type=F32)
            lap = jnp.dot(left_ref[: 2 * rows, :], lap_ref[...], preferred_element_type=F32)
            first_ref[...] += out[:rows] + out[rows : 2 * rows]
            sigma_ref[...] += (out[2 * rows : 3 * rows] + out[3 * rows : 4 * rows]) + (lap[:rows] + lap[rows:])
            v_ref[...] += out[4 * rows : 4 * rows + count] + out[4 * rows + count :]
            return carry

        lax.fori_loop(0, pieces, body, 0)
    if ended:
        for send_ref, top in ((refs[3], False), (refs[4], True)):
            for p in range(probes):
                z = p * count + (count - 8 if top else 0)
                send_ref[8 * p : 8 * p + 8, :] = first_ref[z : z + 8, :]
                z = p * count + (count - 4 if top else 0)
                send_ref[8 * probes + 4 * p : 8 * probes + 4 * p + 4, :] = sigma_ref[z : z + 4, :]
            z = count - 4 if top else 0
            send_ref[12 * probes : 12 * probes + 4, :] = v_ref[z : z + 4, :]
            send_ref[12 * probes + 4 :, :] = jnp.zeros((4, send_ref.shape[1]), F32)


def late_kernel(count, probes, first_ref, sigma_ref, v_ref, low_ref, high_ref, late_ref, f_ref, s_ref, w_ref):
    deep = count + 8
    top = 12 * probes
    w_ref[:4, :] = low_ref[top : top + 4, :]
    w_ref[4 : 4 + count, :] = v_ref[...]
    w_ref[4 + count :, :] = high_ref[top : top + 4, :]
    w = w_ref[...]
    w = w * w
    for p in range(probes):
        f_ref[:8, :] = low_ref[8 * p : 8 * p + 8, :]
        f_ref[8 : 8 + count, :] = first_ref[p * count : (p + 1) * count, :]
        f_ref[8 + count :, :] = high_ref[8 * p : 8 * p + 8, :]
        z = 8 * probes + 4 * p
        s_ref[:4, :] = low_ref[z : z + 4, :]
        s_ref[4 : 4 + count, :] = sigma_ref[p * count : (p + 1) * count, :]
        s_ref[4 + count :, :] = high_ref[z : z + 4, :]
        sigma = SCALE * s_ref[...]
        for k in range(1, 5):
            sigma = sigma + WEIGHTS[k - 1] * (f_ref[4 - k : 4 - k + deep, :] + f_ref[4 + k : 4 + k + deep, :])
        late_ref[p * deep : (p + 1) * deep, :] = w * sigma


def image_kernel(count, probes, flips, scale, started, me_ref, buf_ref, m_ref, *refs):
    n = len(flips)
    late_refs, refs = refs[:n], refs[n:]
    if started:
        start_ref, refs = refs[0], refs[1:]
    out_ref, late_ref, spot_ref, lap_ref, left_ref, matrix_ref = refs
    width = m_ref.shape[1]
    rows = probes * count
    step = pl.program_id(0)
    n_wells = late_ref.shape[1]

    @pl.when(step == 0)
    def _():
        out_ref[...] = start_ref[...] if started else jnp.zeros_like(out_ref)
        matrix_ref[...] = stencil_matrix(width)

    for i in range(n):

        @pl.when(step == i)
        def _(i=i):
            late_ref[...] = late_refs[i][...]

    top = 4 * count * 8
    wells = jnp.concatenate([buf_ref[0, top + i : top + i + 1, :] for i in range(n_wells // width)], axis=1)
    x_row, spot, side = masks_of(wells.astype(jnp.int32), width, matrix_ref[...])
    x_rows = rows_of(x_row, me_ref[0] * 16, 16)
    for p in range(probes):
        top = p * (count + 8)
        here = late_ref[top + 4 : top + 4 + count, :]
        along_z = CENTER * here
        for k in range(1, 5):
            along_z = along_z + WEIGHTS[k - 1] * (
                late_ref[top + 4 - k : top + 4 - k + count, :] + late_ref[top + 4 + k : top + 4 + k + count, :]
            )
        for j, value in enumerate((along_z, here)):
            high, low = halves(value)
            left_ref[2 * j * rows + p * count : 2 * j * rows + (p + 1) * count, :] = high
            left_ref[(2 * j + 1) * rows + p * count : (2 * j + 1) * rows + (p + 1) * count, :] = low
    left_ref[4 * rows :, :] = jnp.ones((count, n_wells), BF16)
    contract = (((1,), (1,)), ((), ()))
    for half in range(2):
        for pair in range(4):
            slot = pair % 2
            for j in range(2):
                x = half * 8 + pair * 2 + j
                fill(x_rows, spot, side, x, spot_ref.at[slot], lap_ref.at[slot], j * width)
            out = lax.dot_general(left_ref[...], spot_ref[slot], contract, preferred_element_type=F32)
            lap = lax.dot_general(left_ref[2 * rows : 4 * rows, :], lap_ref[slot], contract, preferred_element_type=F32)
            field = (out[:rows] + out[rows : 2 * rows]) + SCALE * (lap[:rows] + lap[rows:])
            late = out[2 * rows : 3 * rows] + out[3 * rows : 4 * rows]
            hits = out[4 * rows :]
            for j in range(2):
                x = pair * 2 + j
                columns = slice(j * width, (j + 1) * width)
                born = buf_ref[0, pl.ds(half * count * 8 + x, count, stride=8), :]
                both = buf_ref[0, pl.ds((2 + half) * count * 8 + x, count, stride=8), :]
                seen = hits[:, columns] * born
                m_rows = pl.ds(half * 8 + x, rows, stride=16)
                tile = lambda value: jnp.concatenate([value] * probes, axis=0)
                out_ref[m_rows, :] += (
                    tile(born) * (field[:, columns] + tile(seen) * m_ref[m_rows, :]) + tile(both) * late[:, columns]
                )

    if scale != 1.0:

        @pl.when(step == n - 1)
        def _():
            out_ref[...] = out_ref[...] * scale


VMEM = pl.BlockSpec(memory_space=pltpu.VMEM)
SMEM = pl.BlockSpec(memory_space=pltpu.SMEM)


def spread(low_layers, high_layers, axis="space"):
    count = lax.axis_size(axis)
    forward = [(i, i + 1) for i in range(count - 1)]
    backward = [(i + 1, i) for i in range(count - 1)]
    return lax.ppermute(high_layers, axis, forward), lax.ppermute(low_layers, axis, backward)


def slab(wave_prev, wave_now, velocity, probe_panel, source_depth, source_column, source_strength, receiver_wells):
    count, width = wave_now.shape[1], wave_now.shape[2]
    probes = probe_panel.shape[0]
    strips = lax.axis_size("shot")
    n_wells = receiver_wells.shape[1]
    rows = probes * count
    me = lax.axis_index("shot").reshape(1).astype(jnp.int32)
    params = pltpu.CompilerParams(vmem_limit_bytes=49 * 1024 * 1024)
    gather_params = pltpu.CompilerParams(vmem_limit_bytes=30 * 1024 * 1024)
    image_params = pltpu.CompilerParams(vmem_limit_bytes=67043328)

    rounds = strips // 2
    swap = [(i, i ^ 1) for i in range(strips)]

    def sent(value, pairs):
        return lax.ppermute(value, "shot", pairs)

    def ring(shift):
        return [(i, (i + 2 * shift) % strips) for i in range(strips)]

    now_low, now_high = spread(wave_now[0, :4], wave_now[0, count - 4 :])
    swapped = sent(probe_panel, swap)
    part_b = probe_panel[:, :, 8:]
    b_ring = [sent(part_b, ring(s)) for s in range(1, rounds)]
    a_pair = jnp.stack([probe_panel[:, :, :8], swapped[:, :, :8]])
    a_ring = [sent(a_pair, ring(s)) for s in range(1, rounds)]
    b_stack = jnp.stack(b_ring)
    b_other = sent(b_stack, swap)

    slab_id = lax.axis_index("space").reshape(1).astype(jnp.int32)
    plane = jax.ShapeDtypeStruct((count, width, width), F32)
    edge = jax.ShapeDtypeStruct((4, width, width), F32)
    born, lap, upcoming, up_first, up_last = pl.pallas_call(
        functools.partial(step_kernel, count),
        out_shape=(plane, plane, plane, edge, edge),
        in_specs=[SMEM] * 4 + [VMEM] * 5,
        out_specs=(VMEM,) * 5,
        compiler_params=params,
        name="step_kernel",
    )(slab_id, source_depth, source_column, source_strength, wave_now[0], now_low, now_high, wave_prev[0], velocity)
    up_low, up_high = spread(up_first, up_last)

    buf_rows = 4 * count * 8 + 8
    buf = pl.pallas_call(
        functools.partial(second_kernel, count, strips),
        out_shape=jax.ShapeDtypeStruct((strips, buf_rows, width), F32),
        in_specs=[VMEM] * 6,
        out_specs=VMEM,
        compiler_params=params,
        name="second_kernel",
    )(receiver_wells, upcoming, up_low, up_high, born, lap)
    shared = lax.all_to_all(buf, "shot", 0, 0, tiled=True)

    compact = jax.ShapeDtypeStruct((rows, n_wells), F32)
    compact_v = jax.ShapeDtypeStruct((count, n_wells), F32)
    edge_rows = 12 * probes + 8

    def gather(parts, plans, start=(), ended=False):
        parts = [part.reshape(-1, rows * (16 if plan[0] is None else 8), width) for part, plan in zip(parts, plans)]
        counts = tuple(part.shape[0] for part in parts)
        out_shape = (compact, compact, compact_v)
        if ended:
            out_shape += (jax.ShapeDtypeStruct((edge_rows, n_wells), F32),) * 2
        return pl.pallas_call(
            functools.partial(gather_kernel, count, probes, rounds, plans, counts, bool(start), ended),
            out_shape=out_shape,
            in_specs=[SMEM] + [VMEM] * (3 + len(parts) + len(start)),
            out_specs=(VMEM,) * len(out_shape),
            scratch_shapes=[
                pltpu.VMEM((8 * width, n_wells), BF16),
                pltpu.VMEM((8 * width, n_wells), BF16),
                pltpu.VMEM((4 * rows + 2 * count, 8 * width), BF16),
            ],
            compiler_params=gather_params,
        )(me, receiver_wells, velocity.reshape(count * width, width), buf, *parts, *start)

    own_plans = ((None, 0, 0, 0, 0), (None, 0, 0, 1, 0)) + tuple((1, s, 0, 0, 0) for s in range(1, rounds))
    own = gather([probe_panel, swapped] + b_ring, own_plans)
    first_ring, rest = a_ring[0], a_ring[1:]
    most = gather([first_ring, b_other], ((0, 1, 0, 0, 1), (1, 1, 1, 1, 0)), own)
    last_plans = tuple((0, s, 0, 0, 1) for s in range(2, rounds))
    first, sigma, vel, send_low, send_high = gather(rest, last_plans, most, True)
    low, high = spread(send_low, send_high)
    deep = count + 8
    late = pl.pallas_call(
        functools.partial(late_kernel, count, probes),
        out_shape=jax.ShapeDtypeStruct((probes * deep, n_wells), F32),
        in_specs=[VMEM] * 5,
        out_specs=VMEM,
        scratch_shapes=[
            pltpu.VMEM((count + 16, n_wells), F32),
            pltpu.VMEM((deep, n_wells), F32),
            pltpu.VMEM((deep, n_wells), F32),
        ],
        compiler_params=params,
        name="late_kernel",
    )(first, sigma, vel, low, high)

    late_from = {0: late}
    for flip in NEAR + FAR:
        late_from[flip] = sent(late, [(i, i ^ flip) for i in range(strips)])
    panel = probe_panel.reshape(rows * 16, width)

    def image(source, flips, scale, start=()):
        whole = pl.BlockSpec((rows * 16, width), lambda s, me: (0, 0))

        def shot_block(s, me):
            flip = flips[-1]
            for i in range(len(flips) - 2, -1, -1):
                flip = jnp.where(s == i, flips[i], flip)
            return (me[0] ^ flip, 0, 0)

        return pl.pallas_call(
            functools.partial(image_kernel, count, probes, flips, scale, bool(start)),
            out_shape=jax.ShapeDtypeStruct((rows * 16, width), F32),
            grid_spec=pltpu.PrefetchScalarGridSpec(
                num_scalar_prefetch=1,
                grid=(len(flips),),
                in_specs=[pl.BlockSpec((1, buf_rows, width), shot_block), whole]
                + [pl.BlockSpec((probes * deep, n_wells), lambda s, me: (0, 0))] * len(flips)
                + [whole] * len(start),
                out_specs=whole,
                scratch_shapes=[
                    pltpu.VMEM((probes * deep, n_wells), F32),
                    pltpu.VMEM((2, 2 * width, n_wells), BF16),
                    pltpu.VMEM((2, 2 * width, n_wells), BF16),
                    pltpu.VMEM((4 * rows + count, n_wells), BF16),
                    pltpu.VMEM((width, width), BF16),
                ],
            ),
            compiler_params=image_params,
        )(me, source, panel, *[late_from[flip] for flip in flips], *start)

    total = image(buf, (0,), 1.0)
    total = image(shared, NEAR, 1.0, (total,))
    total = image(shared, FAR, 1.0 / strips, (total,))
    return total.reshape(probe_panel.shape)


NEAR = (1, 2, 6)
FAR = (4, 5, 3, 7)


def solution(mesh):
    return jax.shard_map(
        slab,
        mesh=mesh,
        in_specs=(
            P("shot", "space", None, None),
            P("shot", "space", None, None),
            P("space", None, None),
            P(None, "space", "shot", None),
            P("shot"),
            P("shot"),
            P("shot"),
            P("shot", None),
        ),
        out_specs=P(None, "space", "shot", None),
        check_vma=False,
    )
```
